32 devices in a mesh: gx: 4 (over z), gy: 8 (over y, x, core).
Axes of the slice: x: 2, y: 2, z: 4, core: 2. Of those that a mesh axis runs over, the one named last changes fastest.
Arguments:
- reference_scan: bfloat16 [128, 256, 128], P('gx', 'gy'), may hold values from -6 to 6
- deformed_scan: bfloat16 [128, 256, 128], P('gx', 'gy'), may hold values from -6 to 6
- source_column: int32 [4, 8, 64, 1], P('gx'), may hold values from 0 to 7, as said below
Outputs:
- update: float32 [3, 8, 16, 9], P(None, 'gx', 'gy')
- cg_residual: float32 [3, 8, 16, 9], P(None, 'gx', 'gy')
The draws below stay inside these ranges and needn't reach their ends.
Inputs may be any that keep to these rules, and one draw needn't show every extreme that they name: source_column[p, q, b, 0] is q - 1, q or q + 1. Within one brick's 64 blocks at most 16 come from column q - 1 and at most 16 from column q + 1; in every draw some brick takes exactly 16 blocks from column q - 1 and some brick exactly 16 from column q + 1.
All inputs are finite; a program needn't handle non-finite values.
Results may differ from the reference program's by a relative error of at most 0.0003.
Values may be sent and summed in bfloat16 or wider, within the bound.
No kernel may reach another device: no remote copies, remote signals or barrier semaphores. Data moves between devices by JAX's collectives and lax.ppermute only.
A program may use at most 64 MiB of HBM per device.

```python
import jax
import jax.numpy as jnp
from jax import lax

BX = 32
BY = 32
BZ = 128
E = 16
ITERS = 4
NBLK = 64
CAP = 16
NX = 128
NY = 256
NZN = 9
GNX = 8
GNY = 16
N_GX = 4
N_GY = 8


def draw_source_column(key, part):
    keys = jax.random.split(jax.random.fold_in(key, 17), 7)
    left_count = jax.random.randint(keys[0], (N_GX, N_GY), 0, CAP + 1)
    right_count = jax.random.randint(keys[1], (N_GX, N_GY), 0, CAP + 1)
    rows = jnp.arange(N_GX, dtype=jnp.int32)[:, None]
    cols = jnp.arange(N_GY, dtype=jnp.int32)[None, :]
    left_row = jax.random.randint(keys[2], (), 0, N_GX)
    left_col = jax.random.randint(keys[3], (), 1, N_GY)
    right_row = jax.random.randint(keys[4], (), 0, N_GX)
    right_col = jax.random.randint(keys[5], (), 0, N_GY - 1)
    left_count = jnp.where((rows == left_row) & (cols == left_col), CAP, left_count)
    right_count = jnp.where((rows == right_row) & (cols == right_col), CAP, right_count)
    scores = jax.random.randint(keys[6], (N_GX, N_GY, NBLK), 0, 1 << 20)
    scores = scores * NBLK + jnp.arange(NBLK, dtype=jnp.int32)[None, None, :]
    order = jnp.argsort(scores, axis=2)
    rank = jnp.argsort(order, axis=2).astype(jnp.int32)
    offset = jnp.where(rank < left_count[:, :, None], -1, jnp.where(rank < (left_count + right_count)[:, :, None], 1, 0))
    column = jnp.clip(cols[:, :, None] + offset, 0, N_GY - 1).astype(jnp.int32)
    return column[:, :, :, None]


def shard_levels(key, shape, cuts, low, top_value):
    def one(dim, blocks):
        steps = jax.random.uniform(jax.random.fold_in(jax.random.fold_in(key, 6), dim), (blocks,), jnp.float32, low / len(cuts), top_value / len(cuts))
        return jnp.repeat(jnp.exp(steps), shape[dim] // blocks).reshape((-1,) + (1,) * (len(shape) - dim - 1))

    factor_of = one(*cuts[0])
    for cut in cuts[1:]:
        factor_of = factor_of * one(*cut)
    return factor_of


def noise(own_key, dims, scale, most, cuts=(), kind=jnp.bfloat16):
    values = jax.random.normal(own_key, dims, jnp.float32) * scale
    if len(cuts) > 0:
        values = shard_levels(own_key, dims, cuts, -0.22, 0.18) * values
    return jnp.clip(values, min=-most, max=most).astype(kind)


def setup_inputs(seed: int = 0) -> dict:
    splits = jax.random.split(jax.random.key(seed), 4)
    return {
        "reference_scan": noise(splits[0], (NX, NY, BZ), 1.0, 6.0, ((0, 4), (1, 8))),
        "deformed_scan": noise(splits[1], (NX, NY, BZ), 1.0, 6.0, ((0, 4), (1, 8))),
        "source_column": draw_source_column(jax.random.fold_in(splits[3], 71), 0),
    }


damping = 0.1


def shape_matrix(count, nodes, edge):
    position = jnp.arange(count, dtype=jnp.float32)[:, None]
    anchor = jnp.arange(nodes, dtype=jnp.float32)[None, :] * edge
    return jnp.maximum(0.0, 1.0 - jnp.abs(position - anchor) / edge)


def reference(reference_scan, deformed_scan, source_column):
    blocks = deformed_scan.reshape(N_GX, BX // 8, 8, N_GY, BY // 8, 8, 4, BZ // 4)
    blocks = blocks.transpose(0, 3, 1, 4, 6, 2, 5, 7).reshape(N_GX, N_GY, NBLK, 16 * BZ)
    row_index = jnp.arange(N_GX, dtype=jnp.int32)[:, None, None]
    block_index = jnp.arange(NBLK, dtype=jnp.int32)[None, None, :]
    chosen = blocks[row_index, source_column[:, :, :, 0].astype(jnp.int32), block_index]
    warped = chosen.reshape(N_GX, N_GY, BX // 8, BY // 8, 4, 8, 8, BZ // 4)
    warped = warped.transpose(0, 2, 5, 1, 3, 6, 4, 7).reshape(NX, NY, BZ)
    field = reference_scan.astype(jnp.float32)
    padded = jnp.pad(field, 1)
    scale = 1.0 / (2.0 * E)
    gradient = [
        (padded[2:, 1:-1, 1:-1] - padded[:-2, 1:-1, 1:-1]) * scale,
        (padded[1:-1, 2:, 1:-1] - padded[1:-1, :-2, 1:-1]) * scale,
        (padded[1:-1, 1:-1, 2:] - padded[1:-1, 1:-1, :-2]) * scale,
    ]
    misfit = field - warped.astype(jnp.float32)
    matrix_x = shape_matrix(NX, GNX, float(E))
    matrix_y = shape_matrix(NY, GNY, float(E))
    matrix_z = shape_matrix(BZ, NZN, float(E))
    highest = lax.Precision.HIGHEST

    def spread(nodal):
        temp = jnp.einsum("ijk,zk->ijz", nodal, matrix_z, precision=highest)
        temp = jnp.einsum("ijz,yj->iyz", temp, matrix_y, precision=highest)
        return jnp.einsum("iyz,xi->xyz", temp, matrix_x, precision=highest)

    def collect(voxels):
        temp = jnp.einsum("xyz,xi->iyz", voxels, matrix_x, precision=highest)
        temp = jnp.einsum("iyz,yj->ijz", temp, matrix_y, precision=highest)
        return jnp.einsum("ijz,zk->ijk", temp, matrix_z, precision=highest)

    def operate(nodal):
        along = gradient[0] * spread(nodal[0])
        along = along + gradient[1] * spread(nodal[1])
        along = along + gradient[2] * spread(nodal[2])
        back = jnp.stack([collect(gradient[c] * along) for c in range(3)])
        return back + damping * nodal

    rhs = jnp.stack([collect(gradient[c] * misfit) for c in range(3)])
    update = jnp.zeros_like(rhs)
    residual = rhs
    direction = rhs
    norm_now = jnp.sum(residual * residual)
    for turn in range(ITERS):
        image = operate(direction)
        alpha = norm_now / jnp.sum(direction * image)
        update = update + alpha * direction
        residual = residual - alpha * image
        norm_next = jnp.sum(residual * residual)
        direction = residual + (norm_next / norm_now) * direction
        norm_now = norm_next
    return update, residual
```

```python
import functools

import jax
import jax.numpy as jnp
import numpy as np
from jax import lax
from jax.experimental import pallas as pl
from jax.experimental.pallas import tpu as pltpu
from jax.sharding import PartitionSpec as P

E = 16
ITERS = 4
NZN = 9
OWN = 12 * NZN


damping = 0.1


def weights():
    m = np.arange(E, 0, -1, dtype=np.float64) / E
    same_low, cross, same_high, low, high = m * m, m * (1 - m), (1 - m) ** 2, m, 1 - m

    def along(count):
        d = np.zeros((count + 1, count * E))
        o = np.zeros((count + 1, count * E))
        h = np.zeros((count + 1, count * E))
        for e in range(count):
            at = slice(e * E, (e + 1) * E)
            d[e, at] += same_low
            d[e + 1, at] += same_high
            o[e, at] += cross
            h[e, at] += low
            h[e + 1, at] += high
        return d, o, h

    yd, yo, yh = along(2)
    w = np.zeros((48, 160))
    for s in range(2):
        for tx in range(2):
            k = slice((s * 2 + tx) * 32, (s * 2 + tx) * 32 + 32)
            for iy in range(2):
                w[iy * 8 + s * 4 + tx * 2 + 0, k] = yd[iy]
                w[iy * 8 + s * 4 + tx * 2 + 1, k] = yo[iy]
            w[16 + s * 2 + tx, k] = yd[2]
        k = slice(s * 64, s * 64 + 32)
        for iy in range(2):
            w[24 + iy * 4 + s * 2 + 0, k] = yd[iy]
            w[24 + iy * 4 + s * 2 + 1, k] = yo[iy]
        w[(32 if s == 0 else 40) + 7, k] = yd[2]
    for iy in range(3):
        w[20 + iy, 128:160] = yh[iy]
        w[32 + 4 + iy, 128:160] = yh[iy]
    zd, zo, zh = along(8)
    z = np.zeros((128, 128))
    scale = 1.0 / (2.0 * E)
    z[:, 0:9] = zd.T * scale * scale
    z[:, 9:18] = zo.T * scale * scale
    z[:, 18:27] = zh.T * scale
    return w.astype(np.float32), z.astype(np.float32)


def split3(value):
    high = value.astype(jnp.bfloat16)
    rest = value - high.astype(jnp.float32)
    mid = rest.astype(jnp.bfloat16)
    low = (rest - mid.astype(jnp.float32)).astype(jnp.bfloat16)
    return high, mid, low


def pack_kernel(f_ref, d_ref, ya_ref, yb_ref, xa_ref, xb_ref):
    even_x = lax.rem(lax.axis_index("gx"), 2) == 0
    even_y = lax.rem(lax.axis_index("gy"), 2) == 0
    bx, by, _ = f_ref.shape
    ya_ref[0:bx] = d_ref[...]
    yb_ref[0:bx] = d_ref[...]
    head, tail = f_ref[:, 0, :], f_ref[:, by - 1, :]
    ya_ref[bx] = jnp.where(even_y, tail, head)
    yb_ref[bx] = jnp.where(even_y, head, tail)
    xa_ref[...] = jnp.where(even_x, f_ref[bx - 1], f_ref[0])
    xb_ref[...] = jnp.where(even_x, f_ref[0], f_ref[bx - 1])


PAIRS = ((0, 0), (1, 1), (2, 2), (0, 1), (1, 2), (2, 0))


def assemble_kernel(f_ref, d_ref, ra_ref, rb_ref, xa_ref, xb_ref, col_ref, w_ref, z_ref, out_ref, field, slope, misfit, source, moment):
    px, qy = lax.axis_index("gx"), lax.axis_index("gy")
    even_x, even_y = lax.rem(px, 2) == 0, lax.rem(qy, 2) == 0
    bx, by, bz = f_ref.shape
    f32 = jnp.float32
    lane = lax.broadcasted_iota(jnp.int32, (8, bz), 1)
    sign = jnp.where(even_y, 1, -1)
    for i in range(bx // 8):
        for j in range(by // 8):
            code = jnp.zeros((8, bz), jnp.int32)
            for k in range(4):
                at = (col_ref[qy, (i * (by // 8) + j) * 4 + k] - qy) * sign
                code = jnp.where(lane // (bz // 4) == k, at, code)
            source[i, j * 8 : j * 8 + 8, :] = code
    field[0, 8 : 8 + by, :] = jnp.where(even_x, xb_ref[...], xa_ref[...]).astype(f32)
    field[bx + 1, 8 : 8 + by, :] = jnp.where(even_x, xa_ref[...], xb_ref[...]).astype(f32)
    rim_a, rim_b = ra_ref[bx].astype(f32), rb_ref[bx].astype(f32)
    field[1 : bx + 1, 7, :] = jnp.where(even_y, rim_b, rim_a)
    field[1 : bx + 1, 8 + by, :] = jnp.where(even_y, rim_a, rim_b)

    def prepare(x, _):
        here = f_ref[x].astype(f32)
        field[x + 1, 8 : 8 + by, :] = here
        slope[x] = field[x + 1, 9 : 9 + by, :] - field[x + 1, 7 : 7 + by, :]
        code = source[x // 8]
        warped = jnp.where(code == 0, d_ref[x].astype(f32), jnp.where(code > 0, ra_ref[x].astype(f32), rb_ref[x].astype(f32)))
        misfit[x] = here - warped
        return 0

    lax.fori_loop(0, bx, prepare, 0)

    def group(g, _):
        rows = pl.ds(pl.multiple_of(g * 8, 8), 8)
        rows_f = pl.ds(pl.multiple_of(g * 8 + 8, 8), 8)
        found = []
        for e in range(2):
            before, now = field[e * E, rows_f, :], field[e * E + 1, rows_f, :]
            tot = [[jnp.zeros((8, bz), f32) for _ in range(3)] for _ in range(6)]
            right = [[jnp.zeros((8, bz), f32) for _ in range(2)] for _ in range(3)]
            for t in range(E):
                x = e * E + t
                after = field[x + 2, rows_f, :]
                up = jnp.where(lane == bz - 1, 0.0, pltpu.roll(now, bz - 1, 1))
                down = jnp.where(lane == 0, 0.0, pltpu.roll(now, 1, 1))
                grad = (after - before, slope[x, rows, :], up - down)
                for n, (c, d) in enumerate(PAIRS):
                    tot[n][0] = tot[n][0] + grad[c] * grad[d]
                    tot[n][1] = tot[n][1] + tot[n][0]
                    tot[n][2] = tot[n][2] + tot[n][1]
                miss = misfit[x, rows, :]
                for c in range(3):
                    right[c][0] = right[c][0] + grad[c] * miss
                    right[c][1] = right[c][1] + right[c][0]
                before, now = now, after
            ent = []
            for n in range(6):
                a0, a1, a2 = tot[n]
                sq = 2.0 * a2 - a1
                ent.append((sq * (1 / 256), (16.0 * a1 - sq) * (1 / 256), a0 - a1 * (1 / 8) + sq * (1 / 256)))
            rh = [(right[c][1] * (1 / 16), right[c][0] - right[c][1] * (1 / 16)) for c in range(3)]
            found.append((ent, rh))
        for s in range(2):
            for c in range(3):
                e0, e1 = found[0][0][s * 3 + c], found[1][0][s * 3 + c]
                same = (e0[0], e0[2] + e1[0], e1[2])
                cross = (e0[1], e1[1], jnp.zeros((8, bz), f32))
                for ix in range(3):
                    at = slice((c * 3 + ix) * bz, (c * 3 + ix + 1) * bz)
                    moment[pl.ds(pl.multiple_of(s * 64 + g * 8, 8), 8), at] = same[ix]
                    moment[pl.ds(pl.multiple_of(s * 64 + 32 + g * 8, 8), 8), at] = cross[ix]
        for c in range(3):
            r0, r1 = found[0][1][c], found[1][1][c]
            for ix, value in enumerate((r0[0], r0[1] + r1[0], r1[1])):
                at = slice((c * 3 + ix) * bz, (c * 3 + ix + 1) * bz)
                moment[pl.ds(pl.multiple_of(128 + g * 8, 8), 8), at] = value
        return 0

    lax.fori_loop(0, by // 8, group, 0)

    w = w_ref[...]
    along_y = 0.0
    for part in split3(moment[...]):
        along_y = along_y + jnp.dot(w, part, preferred_element_type=f32)
    stacked = jnp.concatenate(
        [along_y[(24 if ix == 2 else 0) : (48 if ix == 2 else 24), (c * 3 + ix) * bz : (c * 3 + ix + 1) * bz] for c in range(3) for ix in range(3)],
        axis=0,
    )
    z = z_ref[...]
    along_z = 0.0
    for part in split3(stacked):
        along_z = along_z + jnp.dot(part, z, preferred_element_type=f32)

    slot = lane // NZN
    row = lax.broadcasted_iota(jnp.int32, (8, bz), 0)
    rows_out = [jnp.zeros((8, bz), f32) for _ in range(3)]

    def place(group_at, value, src, dst, mask=None):
        shift = ((dst - src) * NZN) % bz
        moved = pltpu.roll(value, shift, 1) if shift else value
        keep = slot == dst
        if mask is not None:
            keep = keep & mask
        rows_out[group_at] = jnp.where(keep, moved, rows_out[group_at])

    for c in range(3):
        for ix in range(2):
            at = (c * 3 + ix) * 24
            base = c * 4 + ix * 2
            v0, v1, v2 = (along_z[at + i * 8 : at + i * 8 + 8] for i in range(3))
            for tz in range(2):
                place(tz, v0, tz, base)
                place(tz, v1, tz, base + 1)
                place(2, v2, tz, base + tz, row < 4)
            place(2, v2, 2, base, (row >= 4) & (row < 7))
        at = (c * 3 + 2) * 24
        v0, v1, v2 = (along_z[at + i * 8 : at + i * 8 + 8] for i in range(3))
        for tz in range(2):
            place(c, v0, tz, 12 + tz, (row < 4) if c == 2 else None)
            place(2, v1, tz, c * 4 + tz, row == 7)
            place(2, v2, tz, c * 4 + 2 + tz, row == 7)
        place(2, v1, 2, c * 4 + 1, (row >= 4) & (row < 7))
        if c == 2:
            for tz in range(2):
                place(2, v0, tz, 12 + tz, row >= 4)
    for i in range(3):
        out_ref[i * 8 : i * 8 + 8, :] = rows_out[i]


def solve_kernel(gx, gy, mine_ref, other_ref, up_ref, res_ref, rows, table, vectors):
    count = gx * gy
    px, qy = lax.axis_index("gx"), lax.axis_index("gy")
    odd = lax.rem(qy, 2)
    f32 = jnp.float32
    for i in range(count // 2):
        rows[:, 2 * i + odd, :] = mine_ref[i]
        rows[:, 2 * i + 1 - odd, :] = other_ref[i]
    shape = (count, 128)
    lane = lax.broadcasted_iota(jnp.int32, shape, 1)
    device = lax.broadcasted_iota(jnp.int32, shape, 0)
    q = lax.rem(device, gy)
    slot = lane // NZN
    own = lane < OWN
    ix1 = lax.rem(slot, 4) >= 2
    iy1 = lax.rem(slot, 2) == 1
    corner = own & (lax.rem(slot, 4) == 0)
    x_low = own & ~ix1
    y_low = own & ~iy1
    first_p, last_p = device < gy, device >= count - gy
    first_q, last_q = q == 0, q == gy - 1

    def lanes(value, shift):
        shift = shift % 128
        return pltpu.roll(value, shift, 1) if shift else value

    def down(value, shift):
        shift = shift % count
        return pltpu.roll(value, shift, 0) if shift else value

    def from_below_x(value):
        return jnp.where(first_p, 0.0, down(value, gy))

    def from_below_y(value):
        return jnp.where(first_q, 0.0, down(value, 1))

    def slots(value, src, dst):
        return lanes(value, (dst - src) * NZN)

    def xp(v):
        return jnp.where(ix1, down(lanes(v, 18), -gy), lanes(v, -18))

    def xm(v):
        return jnp.where(ix1, lanes(v, 18), down(lanes(v, -18), gy))

    def yp(v):
        return jnp.where(iy1, down(lanes(v, 9), -1), lanes(v, -9))

    def ym(v):
        return jnp.where(iy1, lanes(v, 9), down(lanes(v, -9), 1))

    def turn(v, j):
        if j == 1:
            return jnp.where(lane < 72, lanes(v, -36), lanes(v, 72))
        return jnp.where(lane < 36, lanes(v, -72), lanes(v, 36))

    for s in range(2):
        for tx in range(2):
            for ty in range(2):
                for tz in range(2):
                    entry = jnp.where(own, rows[tz * 8 + s * 4 + tx * 2 + ty], 0.0)
                    if ty == 0:
                        spill = slots(rows[16 + s * 2 + tx], tz, 0)
                        entry = entry + from_below_y(jnp.where(y_low, spill, 0.0))
                    if tx == 0:
                        spill = jnp.zeros(shape, f32)
                        for c in range(3):
                            for iy in range(2):
                                moved = slots(rows[c * 8 + iy * 4 + s * 2 + ty], 12 + tz, c * 4 + iy)
                                spill = jnp.where(slot == c * 4 + iy, moved, spill)
                        if ty == 0:
                            both = slots(rows[23], s * 2 + tz, 0)
                            spill = spill + from_below_y(jnp.where(corner, both, 0.0))
                        entry = entry + from_below_x(spill)
                    if tx == 1:
                        entry = jnp.where(last_p & ix1, 0.0, entry)
                    if ty == 1:
                        entry = jnp.where(last_q & iy1, 0.0, entry)
                    for dx in (1, -1) if tx else (0,):
                        by_x = jnp.where(own, xm(entry), 0.0) if dx < 0 else entry
                        for dy in (1, -1) if ty else (0,):
                            by_y = jnp.where(own, ym(by_x), 0.0) if dy < 0 else by_x
                            for dz in (1, -1) if tz else (0,):
                                by_z = lanes(by_y, 1) if dz < 0 else by_y
                                offset = (dx + 1) * 9 + (dy + 1) * 3 + dz + 1
                                if s == 0:
                                    table[offset] = by_z
                                else:
                                    table[54 + offset] = by_z
                                    table[27 + offset] = turn(by_z, 2)

    r0, r1, r2 = rows[20], rows[21], rows[22]
    rhs = jnp.where(iy1, lanes(r1, 9), r0) + from_below_y(jnp.where(iy1, 0.0, r2))
    far = jnp.where(iy1, r1, lanes(r0, -9)) + from_below_y(jnp.where(iy1, 0.0, lanes(r2, -9)))
    rhs = rhs + from_below_x(jnp.where(ix1, 0.0, far))
    rhs = jnp.where(own, rhs, 0.0)

    def operate(v):
        parts = [jnp.zeros(shape, f32) for _ in range(3)]
        for dx in range(-1, 2):
            vx = v if dx == 0 else (xp(v) if dx > 0 else xm(v))
            for dy in range(-1, 2):
                vy = vx if dy == 0 else (yp(vx) if dy > 0 else ym(vx))
                for dz in range(-1, 2):
                    vz = lanes(vy, -dz)
                    offset = (dx + 1) * 9 + (dy + 1) * 3 + dz + 1
                    for s in range(3):
                        parts[s] = parts[s] + table[27 * s + offset] * vz
        coupled = parts[0] + turn(parts[1], 1) + turn(parts[2], 2)
        return damping * v + jnp.where(own, coupled, 0.0)

    def total(v):
        return jnp.sum(jnp.sum(v, axis=0, keepdims=True), axis=1, keepdims=True)

    update = jnp.zeros(shape, f32)
    residual = rhs
    direction = rhs
    norm_now = total(residual * residual)
    for turn_at in range(ITERS):
        image = operate(direction)
        alpha = norm_now / total(direction * image)
        update = update + alpha * direction
        residual = residual - alpha * image
        if turn_at + 1 < ITERS:
            norm_next = total(residual * residual)
            direction = residual + (norm_next / norm_now) * direction
            norm_now = norm_next
    vectors[0] = update
    vectors[1] = residual
    me = px * gy + qy
    for i, ref in enumerate((up_ref, res_ref)):
        line = vectors[i, pl.ds(me, 1), :]
        for c in range(3):
            for ix in range(2):
                for iy in range(2):
                    ref[c, ix, iy : iy + 1, :] = lanes(line, -(c * 4 + ix * 2 + iy) * NZN)[:, :NZN]


VMEM = pl.BlockSpec(memory_space=pltpu.VMEM)
SMEM = pl.BlockSpec(memory_space=pltpu.SMEM)


def matching(axis, start):
    count = lax.axis_size(axis)
    pairs = []
    for i in range(start, count - 1, 2):
        pairs += [(i, i + 1), (i + 1, i)]
    return pairs


def local(reference_scan, deformed_scan, source_column):
    bx, by, bz = reference_scan.shape
    gx, gy = lax.axis_size("gx"), lax.axis_size("gy")
    half = jnp.bfloat16
    ya, yb, xa, xb = pl.pallas_call(
        pack_kernel,
        out_shape=[jax.ShapeDtypeStruct((bx + 1, by, bz), half)] * 2 + [jax.ShapeDtypeStruct((by, bz), half)] * 2,
        in_specs=[VMEM] * 2,
        out_specs=[VMEM] * 4,
        name="pack",
    )(reference_scan, deformed_scan)
    rb = lax.ppermute(yb, "gy", matching("gy", 1))
    qa = lax.ppermute(xa, "gx", matching("gx", 0))
    qb = lax.ppermute(xb, "gx", matching("gx", 1))
    ra = lax.ppermute(ya, "gy", matching("gy", 0))
    w, z = weights()
    payload = pl.pallas_call(
        assemble_kernel,
        out_shape=jax.ShapeDtypeStruct((24, bz), jnp.float32),
        in_specs=[VMEM] * 6 + [SMEM] + [VMEM] * 2,
        out_specs=VMEM,
        scratch_shapes=[
            pltpu.VMEM((bx + 2, by + 16, bz), jnp.float32),
            pltpu.VMEM((bx, by, bz), jnp.float32),
            pltpu.VMEM((bx, by, bz), jnp.float32),
            pltpu.VMEM((bx // 8, by, bz), jnp.int32),
            pltpu.VMEM((160, 9 * bz), jnp.float32),
        ],
        name="assemble",
    )(reference_scan, deformed_scan, ra, rb, qa, qb, source_column[0, :, :, 0], jnp.asarray(w, half), jnp.asarray(z, half))
    groups = [[i * 2 + core for i in range(gx * gy // 2)] for core in range(2)]
    mine = lax.all_to_all(jnp.broadcast_to(payload[None], (gx * gy // 2, 24, bz)), ("gx", "gy"), 0, 0, axis_index_groups=groups)
    other = lax.ppermute(mine, "gy", [(i, i ^ 1) for i in range(gy)])
    out = jax.ShapeDtypeStruct((3, 2, 2, NZN), jnp.float32)
    update, residual = pl.pallas_call(
        functools.partial(solve_kernel, gx, gy),
        out_shape=[out, out],
        in_specs=[VMEM] * 2,
        out_specs=[VMEM] * 2,
        scratch_shapes=[
            pltpu.VMEM((24, gx * gy, bz), jnp.float32),
            pltpu.VMEM((81, gx * gy, bz), jnp.float32),
            pltpu.VMEM((2, gx * gy, bz), jnp.float32),
        ],
        name="solve",
    )(mine, other)
    return update, residual


def solution(mesh):
    return jax.shard_map(
        local,
        mesh=mesh,
        in_specs=(P("gx", "gy", None), P("gx", "gy", None), P("gx", None, None, None)),
        out_specs=(P(None, "gx", "gy", None), P(None, "gx", "gy", None)),
        check_vma=False,
    )
```

```python
import functools

import jax
import jax.numpy as jnp
import numpy as np
from jax import lax
from jax.experimental import pallas as pl
from jax.experimental.pallas import tpu as pltpu
from jax.sharding import PartitionSpec as P

E = 16
ITERS = 4
NZN = 9
OWN = 12 * NZN


damping = 0.1


def weights():
    m = np.arange(E, 0, -1, dtype=np.float64) / E
    same_low, cross, same_high, low, high = m * m, m * (1 - m), (1 - m) ** 2, m, 1 - m

    def along(count):
        d = np.zeros((count + 1, count * E))
        o = np.zeros((count + 1, count * E))
        h = np.zeros((count + 1, count * E))
        for e in range(count):
            at = slice(e * E, (e + 1) * E)
            d[e, at] += same_low
            d[e + 1, at] += same_high
            o[e, at] += cross
            h[e, at] += low
            h[e + 1, at] += high
        return d, o, h

    yd, yo, yh = along(2)
    w = np.zeros((48, 160))
    for s in range(2):
        for tx in range(2):
            k = slice((s * 2 + tx) * 32, (s * 2 + tx) * 32 + 32)
            for iy in range(2):
                w[iy * 8 + s * 4 + tx * 2 + 0, k] = yd[iy]
                w[iy * 8 + s * 4 + tx * 2 + 1, k] = yo[iy]
            w[16 + s * 2 + tx, k] = yd[2]
        k = slice(s * 64, s * 64 + 32)
        for iy in range(2):
            w[24 + iy * 4 + s * 2 + 0, k] = yd[iy]
            w[24 + iy * 4 + s * 2 + 1, k] = yo[iy]
        w[(32 if s == 0 else 40) + 7, k] = yd[2]
    for iy in range(3):
        w[20 + iy, 128:160] = yh[iy]
        w[32 + 4 + iy, 128:160] = yh[iy]
    zd, zo, zh = along(8)
    z = np.zeros((128, 128))
    scale = 1.0 / (2.0 * E)
    z[:, 0:9] = zd.T * scale * scale
    z[:, 9:18] = zo.T * scale * scale
    z[:, 18:27] = zh.T * scale
    return w.astype(np.float32), z.astype(np.float32)


def split3(value):
    high = value.astype(jnp.bfloat16)
    rest = value - high.astype(jnp.float32)
    mid = rest.astype(jnp.bfloat16)
    low = (rest - mid.astype(jnp.float32)).astype(jnp.bfloat16)
    return high, mid, low


def pack_kernel(f_ref, ya_ref, yb_ref, xa_ref, xb_ref):
    even_x = lax.rem(lax.axis_index("gx"), 2) == 0
    even_y = lax.rem(lax.axis_index("gy"), 2) == 0
    bx, by, _ = f_ref.shape
    head, tail = f_ref[:, 0, :], f_ref[:, by - 1, :]
    ya_ref[...] = jnp.where(even_y, tail, head)
    yb_ref[...] = jnp.where(even_y, head, tail)
    xa_ref[...] = jnp.where(even_x, f_ref[bx - 1], f_ref[0])
    xb_ref[...] = jnp.where(even_x, f_ref[0], f_ref[bx - 1])


PAIRS = ((0, 0), (1, 1), (2, 2), (0, 1), (1, 2), (2, 0))


def along_lanes(now, lane):
    size = now.shape[-1]
    up = jnp.where(lane == size - 1, 0.0, pltpu.roll(now, size - 1, 1))
    return up - jnp.where(lane == 0, 0.0, pltpu.roll(now, 1, 1))


def interior_kernel(f_ref, d_ref, ra_ref, rb_ref, ya_ref, yb_ref, col_ref, moment, edge, field, slope, misfit, source):
    qy = lax.axis_index("gy")
    even_y = lax.rem(qy, 2) == 0
    bx, by, bz = f_ref.shape
    f32 = jnp.float32
    lane = lax.broadcasted_iota(jnp.int32, (8, bz), 1)
    sign = jnp.where(even_y, 1, -1)
    for i in range(bx // 8):
        for j in range(by // 8):
            code = jnp.zeros((8, bz), jnp.int32)
            for k in range(4):
                at = (col_ref[qy, (i * (by // 8) + j) * 4 + k] - qy) * sign
                code = jnp.where(lane // (bz // 4) == k, at, code)
            source[i, j * 8 : j * 8 + 8, :] = code
    rim_a, rim_b = ya_ref[...].astype(f32), yb_ref[...].astype(f32)
    field[:, 7, :] = jnp.where(even_y, rim_b, rim_a)
    field[:, 8 + by, :] = jnp.where(even_y, rim_a, rim_b)

    def prepare(x, _):
        field[x, 8 : 8 + by, :] = f_ref[x].astype(f32)
        slope[x] = field[x, 9 : 9 + by, :] - field[x, 7 : 7 + by, :]
        code = source[x // 8]
        warped = jnp.where(code == 0, d_ref[x].astype(f32), jnp.where(code > 0, ra_ref[x].astype(f32), rb_ref[x].astype(f32)))
        misfit[x] = field[x, 8 : 8 + by, :] - warped
        return 0

    lax.fori_loop(0, bx, prepare, 0, unroll=4)
    for i, x in enumerate((0, bx - 1)):
        edge[2 * i] = slope[x]
        edge[2 * i + 1] = misfit[x]

    def group(g, _):
        rows = pl.ds(pl.multiple_of(g * 8, 8), 8)
        rows_f = pl.ds(pl.multiple_of(g * 8 + 8, 8), 8)
        found = []
        for e in range(2):
            first = e * E + (1 if e == 0 else 0)
            last = e * E + E - (2 if e == 1 else 1)
            before, now = field[first - 1, rows_f, :], field[first, rows_f, :]
            tot = [[jnp.zeros((8, bz), f32) for _ in range(3)] for _ in range(6)]
            right = [[jnp.zeros((8, bz), f32) for _ in range(2)] for _ in range(3)]
            for x in range(first, last + 1):
                after = field[x + 1, rows_f, :]
                grad = (after - before, slope[x, rows, :], along_lanes(now, lane))
                for n, (c, d) in enumerate(PAIRS):
                    tot[n][0] = tot[n][0] + grad[c] * grad[d]
                    tot[n][1] = tot[n][1] + tot[n][0]
                    tot[n][2] = tot[n][2] + tot[n][1]
                miss = misfit[x, rows, :]
                for c in range(3):
                    right[c][0] = right[c][0] + grad[c] * miss
                    right[c][1] = right[c][1] + right[c][0]
                before, now = now, after
            if e == 1:
                for n in range(6):
                    tot[n][1] = tot[n][1] + tot[n][0]
                    tot[n][2] = tot[n][2] + tot[n][1]
                for c in range(3):
                    right[c][1] = right[c][1] + right[c][0]
            ent = []
            for n in range(6):
                a0, a1, a2 = tot[n]
                sq = 2.0 * a2 - a1
                ent.append((sq * (1 / 256), (16.0 * a1 - sq) * (1 / 256), a0 - a1 * (1 / 8) + sq * (1 / 256)))
            rh = [(right[c][1] * (1 / 16), right[c][0] - right[c][1] * (1 / 16)) for c in range(3)]
            found.append((ent, rh))
        for s in range(2):
            for c in range(3):
                e0, e1 = found[0][0][s * 3 + c], found[1][0][s * 3 + c]
                same = (e0[0], e0[2] + e1[0], e1[2])
                cross = (e0[1], e1[1], jnp.zeros((8, bz), f32))
                for ix in range(3):
                    at = slice((c * 3 + ix) * bz, (c * 3 + ix + 1) * bz)
                    moment[pl.ds(pl.multiple_of(s * 64 + g * 8, 8), 8), at] = same[ix]
                    moment[pl.ds(pl.multiple_of(s * 64 + 32 + g * 8, 8), 8), at] = cross[ix]
        for c in range(3):
            r0, r1 = found[0][1][c], found[1][1][c]
            for ix, value in enumerate((r0[0], r0[1] + r1[0], r1[1])):
                at = slice((c * 3 + ix) * bz, (c * 3 + ix + 1) * bz)
                moment[pl.ds(pl.multiple_of(128 + g * 8, 8), 8), at] = value
        return 0

    lax.fori_loop(0, by // 8, group, 0)


def finish_kernel(f_ref, xa_ref, xb_ref, edge, moment, w_ref, z_ref, out_ref):
    even_x = lax.rem(lax.axis_index("gx"), 2) == 0
    bx, by, bz = f_ref.shape
    f32 = jnp.float32
    low = jnp.where(even_x, xb_ref[...], xa_ref[...]).astype(f32)
    high = jnp.where(even_x, xa_ref[...], xb_ref[...]).astype(f32)
    lane = lax.broadcasted_iota(jnp.int32, (by, bz), 1)
    planes = []
    for i, (x, before, after) in enumerate(((0, low, f_ref[1].astype(f32)), (bx - 1, f_ref[bx - 2].astype(f32), high))):
        grad = (after - before, edge[2 * i], along_lanes(f_ref[x].astype(f32), lane))
        planes.append(([grad[c] * grad[d] for c, d in PAIRS], [grad[c] * edge[2 * i + 1] for c in range(3)]))
    w = w_ref[...]
    along_y = []
    for c in range(3):
        tiles = []
        for ix in range(3):
            tile = moment[:, (c * 3 + ix) * bz : (c * 3 + ix + 1) * bz]
            pieces = []
            for s in range(2):
                first, last = planes[0][0][s * 3 + c], planes[1][0][s * 3 + c]
                same, cross = tile[s * 64 : s * 64 + 32], tile[s * 64 + 32 : s * 64 + 64]
                if ix == 0:
                    same = same + first
                elif ix == 1:
                    same, cross = same + last * (1 / 256), cross + last * (15 / 256)
                else:
                    same = same + last * (225 / 256)
                pieces += [same, cross]
            first, last = planes[0][1][c], planes[1][1][c]
            pieces.append(tile[128:160] + (first, last * (1 / 16), last * (15 / 16))[ix])
            tiles.append(jnp.concatenate(pieces, axis=0))
        sums = 0.0
        for part in split3(jnp.concatenate(tiles, axis=1)):
            sums = sums + jnp.dot(w, part, preferred_element_type=f32)
        along_y.append(sums)
    stacked = jnp.concatenate(
        [along_y[c][(24 if ix == 2 else 0) : (48 if ix == 2 else 24), ix * bz : (ix + 1) * bz] for c in range(3) for ix in range(3)],
        axis=0,
    )
    z = z_ref[...]
    along_z = 0.0
    for part in split3(stacked):
        along_z = along_z + jnp.dot(part, z, preferred_element_type=f32)

    slot = lax.broadcasted_iota(jnp.int32, (8, bz), 1) // NZN
    row = lax.broadcasted_iota(jnp.int32, (8, bz), 0)
    rows_out = [jnp.zeros((8, bz), f32) for _ in range(3)]

    def place(group_at, value, src, dst, mask=None):
        shift = ((dst - src) * NZN) % bz
        moved = pltpu.roll(value, shift, 1) if shift else value
        keep = slot == dst
        if mask is not None:
            keep = keep & mask
        rows_out[group_at] = jnp.where(keep, moved, rows_out[group_at])

    for c in range(3):
        for ix in range(2):
            at = (c * 3 + ix) * 24
            base = c * 4 + ix * 2
            v0, v1, v2 = (along_z[at + i * 8 : at + i * 8 + 8] for i in range(3))
            for tz in range(2):
                place(tz, v0, tz, base)
                place(tz, v1, tz, base + 1)
                place(2, v2, tz, base + tz, row < 4)
            place(2, v2, 2, base, (row >= 4) & (row < 7))
        at = (c * 3 + 2) * 24
        v0, v1, v2 = (along_z[at + i * 8 : at + i * 8 + 8] for i in range(3))
        for tz in range(2):
            place(c, v0, tz, 12 + tz, (row < 4) if c == 2 else None)
            place(2, v1, tz, c * 4 + tz, row == 7)
            place(2, v2, tz, c * 4 + 2 + tz, row == 7)
        place(2, v1, 2, c * 4 + 1, (row >= 4) & (row < 7))
        if c == 2:
            for tz in range(2):
                place(2, v0, tz, 12 + tz, row >= 4)
    for i in range(3):
        for copy in range(out_ref.shape[0]):
            out_ref[copy, i * 8 : i * 8 + 8, :] = rows_out[i]


def solve_kernel(gx, gy, mine_ref, other_ref, up_ref, res_ref, table, vectors):
    count, half, step = gx * gy, gx * gy // 2, gy // 2
    px, qy = lax.axis_index("gx"), lax.axis_index("gy")
    odd = lax.rem(qy, 2)
    f32 = jnp.float32
    shape = (count, 128)
    lane = lax.broadcasted_iota(jnp.int32, shape, 1)
    device = lax.broadcasted_iota(jnp.int32, shape, 0)
    core = device >= half
    place = jnp.where(core, device - half, device)
    chip = lax.rem(place, step)
    slot = lane // NZN
    own = lane < OWN
    ix1 = lax.rem(slot, 4) >= 2
    iy1 = lax.rem(slot, 2) == 1
    corner = own & (lax.rem(slot, 4) == 0)
    y_low = own & ~iy1
    first_p, last_p = place < step, place >= half - step
    first_q, last_q = (chip == 0) & ~core, (chip == step - 1) & core
    is_odd = jnp.full((half, 128), odd, jnp.int32) == 1

    def row(r):
        a, b = mine_ref[pl.ds(r, half, stride=24), :], other_ref[pl.ds(r, half, stride=24), :]
        return jnp.concatenate([jnp.where(is_odd, b, a), jnp.where(is_odd, a, b)], axis=0)

    rows = [row(r) for r in range(24)]

    def lanes(value, shift):
        shift = shift % 128
        return pltpu.roll(value, shift, 1) if shift else value

    def down(value, shift):
        shift = shift % value.shape[0]
        return pltpu.roll(value, shift, 0) if shift else value

    def next_x(value, sign):
        return down(value, -sign * step)

    def next_y(value, sign):
        low, high = value[:half], value[half:]
        if sign > 0:
            return jnp.concatenate([high, down(low, -1)], axis=0)
        return jnp.concatenate([down(high, 1), low], axis=0)

    def from_below_x(value):
        return jnp.where(first_p, 0.0, next_x(value, -1))

    def from_below_y(value):
        return jnp.where(first_q, 0.0, next_y(value, -1))

    def slots(value, src, dst):
        return lanes(value, (dst - src) * NZN)

    def xp(v):
        return jnp.where(ix1, next_x(lanes(v, 18), 1), lanes(v, -18))

    def xm(v):
        return jnp.where(ix1, lanes(v, 18), next_x(lanes(v, -18), -1))

    def yp(v):
        return jnp.where(iy1, next_y(lanes(v, 9), 1), lanes(v, -9))

    def ym(v):
        return jnp.where(iy1, lanes(v, 9), next_y(lanes(v, -9), -1))

    def turn(v, j):
        if j == 1:
            return jnp.where(lane < 72, lanes(v, -36), lanes(v, 72))
        return jnp.where(lane < 36, lanes(v, -72), lanes(v, 36))

    for s in range(2):
        for tx in range(2):
            for ty in range(2):
                for tz in range(2):
                    entry = jnp.where(own, rows[tz * 8 + s * 4 + tx * 2 + ty], 0.0)
                    if ty == 0:
                        spill = slots(rows[16 + s * 2 + tx], tz, 0)
                        entry = entry + from_below_y(jnp.where(y_low, spill, 0.0))
                    if tx == 0:
                        spill = jnp.zeros(shape, f32)
                        for c in range(3):
                            for iy in range(2):
                                moved = slots(rows[c * 8 + iy * 4 + s * 2 + ty], 12 + tz, c * 4 + iy)
                                spill = jnp.where(slot == c * 4 + iy, moved, spill)
                        if ty == 0:
                            both = slots(rows[23], s * 2 + tz, 0)
                            spill = spill + from_below_y(jnp.where(corner, both, 0.0))
                        entry = entry + from_below_x(spill)
                    if tx == 1:
                        entry = jnp.where(last_p & ix1, 0.0, entry)
                    if ty == 1:
                        entry = jnp.where(last_q & iy1, 0.0, entry)
                    kind = tx * 4 + ty * 2 + tz
                    if s == 0:
                        table[kind] = entry
                    else:
                        table[8 + kind] = jnp.where(own, turn(entry, 2), 0.0)
                        table[16 + kind] = entry

    r0, r1, r2 = rows[20], rows[21], rows[22]
    rhs = jnp.where(iy1, lanes(r1, 9), r0) + from_below_y(jnp.where(iy1, 0.0, r2))
    far = jnp.where(iy1, r1, lanes(r0, -9)) + from_below_y(jnp.where(iy1, 0.0, lanes(r2, -9)))
    rhs = rhs + from_below_x(jnp.where(ix1, 0.0, far))
    rhs = jnp.where(own, rhs, 0.0)

    def operate(v):
        upper = [v, lanes(v, -1)]
        upper += [yp(u) for u in upper]
        upper += [xp(u) for u in upper]
        parts = []
        for s in range(3):
            low = []
            for to in range(8):
                found = 0.0
                for up in range(8):
                    if up & to == 0:
                        found = found + table[8 * s + (up | to)] * upper[up]
                low.append(found)
            by_z = [low[2 * i] + lanes(low[2 * i + 1], 1) for i in range(4)]
            by_y = [by_z[2 * i] + ym(by_z[2 * i + 1]) for i in range(2)]
            parts.append(by_y[0] + xm(by_y[1]))
        coupled = parts[0] + turn(parts[1], 1) + turn(parts[2], 2)
        return damping * v + jnp.where(own, coupled, 0.0)

    def total(v):
        return jnp.sum(jnp.sum(v, axis=0, keepdims=True), axis=1, keepdims=True)

    def iterate(_, state):
        update, residual, direction, norm_now = state
        image = operate(direction)
        alpha = norm_now / total(direction * image)
        update = update + alpha * direction
        residual = residual - alpha * image
        norm_next = total(residual * residual)
        direction = residual + (norm_next / norm_now) * direction
        return update, residual, direction, norm_next

    start = (jnp.zeros(shape, f32), rhs, rhs, total(rhs * rhs))
    for turn_at in range(ITERS):
        start = iterate(turn_at, start)
    update, residual, _, _ = start
    vectors[0] = update
    vectors[1] = residual
    me = odd * half + px * step + qy // 2
    for i, ref in enumerate((up_ref, res_ref)):
        line = vectors[i, pl.ds(me, 1), :]
        for c in range(3):
            for ix in range(2):
                for iy in range(2):
                    ref[c, ix, iy : iy + 1, :] = lanes(line, -(c * 4 + ix * 2 + iy) * NZN)[:, :NZN]


LIMIT = 24 * 2**20
VMEM = pl.BlockSpec(memory_space=pltpu.VMEM)
SMEM = pl.BlockSpec(memory_space=pltpu.SMEM)


def matching(axis, start):
    count = lax.axis_size(axis)
    pairs = []
    for i in range(start, count - 1, 2):
        pairs += [(i, i + 1), (i + 1, i)]
    return pairs


def local(reference_scan, deformed_scan, source_column):
    bx, by, bz = reference_scan.shape
    gx, gy = lax.axis_size("gx"), lax.axis_size("gy")
    half = jnp.bfloat16
    rb = lax.ppermute(deformed_scan, "gy", matching("gy", 1))
    ra = lax.ppermute(deformed_scan, "gy", matching("gy", 0))
    ya, yb, xa, xb = pl.pallas_call(
        pack_kernel,
        out_shape=[jax.ShapeDtypeStruct((bx, bz), half)] * 2 + [jax.ShapeDtypeStruct((by, bz), half)] * 2,
        in_specs=[VMEM],
        out_specs=[VMEM] * 4,
        compiler_params=pltpu.CompilerParams(vmem_limit_bytes=LIMIT),
        name="pack",
    )(reference_scan)
    yb = lax.ppermute(yb, "gy", matching("gy", 1))
    ya = lax.ppermute(ya, "gy", matching("gy", 0))
    xa = lax.ppermute(xa, "gx", matching("gx", 0))
    xb = lax.ppermute(xb, "gx", matching("gx", 1))
    moment, edge = pl.pallas_call(
        interior_kernel,
        out_shape=[jax.ShapeDtypeStruct((160, 9 * bz), jnp.float32), jax.ShapeDtypeStruct((4, by, bz), jnp.float32)],
        in_specs=[VMEM] * 6 + [SMEM],
        out_specs=[VMEM] * 2,
        scratch_shapes=[
            pltpu.VMEM((bx, by + 16, bz), jnp.float32),
            pltpu.VMEM((bx, by, bz), jnp.float32),
            pltpu.VMEM((bx, by, bz), jnp.float32),
            pltpu.VMEM((bx // 8, by, bz), jnp.int32),
        ],
        compiler_params=pltpu.CompilerParams(vmem_limit_bytes=LIMIT),
        cost_estimate=pl.CostEstimate(flops=8_000_000, bytes_accessed=2_000_000, transcendentals=0),
        name="interior",
    )(reference_scan, deformed_scan, ra, rb, ya, yb, source_column[0, :, :, 0])
    w, z = weights()
    payload = pl.pallas_call(
        finish_kernel,
        out_shape=jax.ShapeDtypeStruct((gx * gy // 2, 24, bz), jnp.float32),
        in_specs=[VMEM] * 7,
        out_specs=VMEM,
        compiler_params=pltpu.CompilerParams(vmem_limit_bytes=LIMIT),
        name="finish",
    )(reference_scan, xa, xb, edge, moment, jnp.asarray(w, half), jnp.asarray(z, half))
    groups = [[i * 2 + core for i in range(gx * gy // 2)] for core in range(2)]
    mine = lax.all_to_all(payload, ("gx", "gy"), 0, 0, axis_index_groups=groups)
    other = lax.ppermute(mine, "gy", [(i, i ^ 1) for i in range(gy)])
    out = jax.ShapeDtypeStruct((3, 2, 2, NZN), jnp.float32)
    update, residual = pl.pallas_call(
        functools.partial(solve_kernel, gx, gy),
        out_shape=[out, out],
        in_specs=[VMEM] * 2,
        out_specs=[VMEM] * 2,
        scratch_shapes=[
            pltpu.VMEM((24, gx * gy, bz), jnp.float32),
            pltpu.VMEM((2, gx * gy, bz), jnp.float32),
        ],
        compiler_params=pltpu.CompilerParams(vmem_limit_bytes=LIMIT),
        name="solve",
    )(mine.reshape(-1, bz), other.reshape(-1, bz))
    return update, residual


def solution(mesh):
    return jax.shard_map(
        local,
        mesh=mesh,
        in_specs=(P("gx", "gy", None), P("gx", "gy", None), P("gx", None, None, None)),
        out_specs=(P(None, "gx", "gy", None), P(None, "gx", "gy", None)),
        check_vma=False,
    )
```

```python
import functools

import jax
import jax.numpy as jnp
import numpy as np
from jax import lax
from jax.experimental import pallas as pl
from jax.experimental.pallas import tpu as pltpu
from jax.sharding import PartitionSpec as P

E = 16
ITERS = 4
NZN = 9
OWN = 12 * NZN


damping = 0.1


def weights():
    m = np.arange(E, 0, -1, dtype=np.float64) / E
    same_low, cross, same_high, low, high = m * m, m * (1 - m), (1 - m) ** 2, m, 1 - m

    def along(count):
        d = np.zeros((count + 1, count * E))
        o = np.zeros((count + 1, count * E))
        h = np.zeros((count + 1, count * E))
        for e in range(count):
            at = slice(e * E, (e + 1) * E)
            d[e, at] += same_low
            d[e + 1, at] += same_high
            o[e, at] += cross
            h[e, at] += low
            h[e + 1, at] += high
        return d, o, h

    yd, yo, yh = along(2)
    w = np.zeros((48, 160))
    for s in range(2):
        for tx in range(2):
            k = slice((s * 2 + tx) * 32, (s * 2 + tx) * 32 + 32)
            for iy in range(2):
                w[iy * 8 + s * 4 + tx * 2 + 0, k] = yd[iy]
                w[iy * 8 + s * 4 + tx * 2 + 1, k] = yo[iy]
            w[16 + s * 2 + tx, k] = yd[2]
        k = slice(s * 64, s * 64 + 32)
        for iy in range(2):
            w[24 + iy * 4 + s * 2 + 0, k] = yd[iy]
            w[24 + iy * 4 + s * 2 + 1, k] = yo[iy]
        w[(32 if s == 0 else 40) + 7, k] = yd[2]
    for iy in range(3):
        w[20 + iy, 128:160] = yh[iy]
        w[32 + 4 + iy, 128:160] = yh[iy]
    zd, zo, zh = along(8)
    z = np.zeros((128, 128))
    scale = 1.0 / (2.0 * E)
    z[:, 0:9] = zd.T * scale * scale
    z[:, 9:18] = zo.T * scale * scale
    z[:, 18:27] = zh.T * scale
    return w.astype(np.float32), z.astype(np.float32)


def split3(value):
    high = value.astype(jnp.bfloat16)
    rest = value - high.astype(jnp.float32)
    mid = rest.astype(jnp.bfloat16)
    low = (rest - mid.astype(jnp.float32)).astype(jnp.bfloat16)
    return high, mid, low


def pack_kernel(f_ref, ya_ref, yb_ref, xa_ref, xb_ref):
    even_x = lax.rem(lax.axis_index("gx"), 2) == 0
    even_y = lax.rem(lax.axis_index("gy"), 2) == 0
    bx, by, _ = f_ref.shape
    head, tail = f_ref[:, 0, :], f_ref[:, by - 1, :]
    ya_ref[...] = jnp.where(even_y, tail, head)
    yb_ref[...] = jnp.where(even_y, head, tail)
    xa_ref[...] = jnp.where(even_x, f_ref[bx - 1], f_ref[0])
    xb_ref[...] = jnp.where(even_x, f_ref[0], f_ref[bx - 1])


PAIRS = ((0, 0), (1, 1), (2, 2), (0, 1), (1, 2), (2, 0))


def along_lanes(now, lane):
    size = now.shape[-1]
    up = jnp.where(lane == size - 1, 0.0, pltpu.roll(now, size - 1, 1))
    return up - jnp.where(lane == 0, 0.0, pltpu.roll(now, 1, 1))


def interior_kernel(gy, f_ref, d_ref, ra_ref, rb_ref, ya_ref, yb_ref, col_ref, moment, edge, field, slope, misfit, source):
    qy = lax.axis_index("gy")
    even_y = lax.rem(qy, 2) == 0
    bx, by, bz = f_ref.shape
    f32 = jnp.float32
    lane = lax.broadcasted_iota(jnp.int32, (8, bz), 1)
    sign = jnp.where(even_y, 1, -1)
    for i in range(bx // 8):
        for j in range(by // 8):
            code = jnp.zeros((8, bz), jnp.int32)
            for k in range(4):
                at = (col_ref[qy, (i * (by // 8) + j) * 4 + k] - qy) * sign
                code = jnp.where(lane // (bz // 4) == k, at, code)
            source[i, j * 8 : j * 8 + 8, :] = code
    rim_a, rim_b = ya_ref[...].astype(f32), yb_ref[...].astype(f32)
    rim_low, rim_high = jnp.where(even_y, rim_b, rim_a), jnp.where(even_y, rim_a, rim_b)
    field[:, 7, :] = jnp.where(qy == 0, 0.0, rim_low)
    field[:, 8 + by, :] = jnp.where(qy == gy - 1, 0.0, rim_high)

    def prepare(x, _):
        field[x, 8 : 8 + by, :] = f_ref[x].astype(f32)
        slope[x] = field[x, 9 : 9 + by, :] - field[x, 7 : 7 + by, :]
        code = source[x // 8]
        warped = jnp.where(code == 0, d_ref[x].astype(f32), jnp.where(code > 0, ra_ref[x].astype(f32), rb_ref[x].astype(f32)))
        misfit[x] = field[x, 8 : 8 + by, :] - warped
        return 0

    lax.fori_loop(0, bx, prepare, 0, unroll=4)
    for i, x in enumerate((0, bx - 1)):
        edge[2 * i] = slope[x]
        edge[2 * i + 1] = misfit[x]

    def group(g, _):
        rows = pl.ds(pl.multiple_of(g * 8, 8), 8)
        rows_f = pl.ds(pl.multiple_of(g * 8 + 8, 8), 8)
        found = []
        for e in range(2):
            first = e * E + (1 if e == 0 else 0)
            last = e * E + E - (2 if e == 1 else 1)
            before, now = field[first - 1, rows_f, :], field[first, rows_f, :]
            tot = [[jnp.zeros((8, bz), f32) for _ in range(3)] for _ in range(6)]
            right = [[jnp.zeros((8, bz), f32) for _ in range(2)] for _ in range(3)]
            for x in range(first, last + 1):
                after = field[x + 1, rows_f, :]
                grad = (after - before, slope[x, rows, :], along_lanes(now, lane))
                for n, (c, d) in enumerate(PAIRS):
                    tot[n][0] = tot[n][0] + grad[c] * grad[d]
                    tot[n][1] = tot[n][1] + tot[n][0]
                    tot[n][2] = tot[n][2] + tot[n][1]
                miss = misfit[x, rows, :]
                for c in range(3):
                    right[c][0] = right[c][0] + grad[c] * miss
                    right[c][1] = right[c][1] + right[c][0]
                before, now = now, after
            if e == 1:
                for n in range(6):
                    tot[n][1] = tot[n][1] + tot[n][0]
                    tot[n][2] = tot[n][2] + tot[n][1]
                for c in range(3):
                    right[c][1] = right[c][1] + right[c][0]
            ent = []
            for n in range(6):
                a0, a1, a2 = tot[n]
                sq = 2.0 * a2 - a1
                ent.append((sq * (1 / 256), (16.0 * a1 - sq) * (1 / 256), a0 - a1 * (1 / 8) + sq * (1 / 256)))
            rh = [(right[c][1] * (1 / 16), right[c][0] - right[c][1] * (1 / 16)) for c in range(3)]
            found.append((ent, rh))
        for s in range(2):
            for c in range(3):
                e0, e1 = found[0][0][s * 3 + c], found[1][0][s * 3 + c]
                same = (e0[0], e0[2] + e1[0], e1[2])
                cross = (e0[1], e1[1], jnp.zeros((8, bz), f32))
                for ix in range(3):
                    at = slice((c * 3 + ix) * bz, (c * 3 + ix + 1) * bz)
                    moment[pl.ds(pl.multiple_of(s * 64 + g * 8, 8), 8), at] = same[ix]
                    moment[pl.ds(pl.multiple_of(s * 64 + 32 + g * 8, 8), 8), at] = cross[ix]
        for c in range(3):
            r0, r1 = found[0][1][c], found[1][1][c]
            for ix, value in enumerate((r0[0], r0[1] + r1[0], r1[1])):
                at = slice((c * 3 + ix) * bz, (c * 3 + ix + 1) * bz)
                moment[pl.ds(pl.multiple_of(128 + g * 8, 8), 8), at] = value
        return 0

    lax.fori_loop(0, by // 8, group, 0)


def finish_kernel(gx, f_ref, xa_ref, xb_ref, edge, moment, w_ref, z_ref, out_ref):
    px = lax.axis_index("gx")
    even_x = lax.rem(px, 2) == 0
    bx, by, bz = f_ref.shape
    f32 = jnp.float32
    low = jnp.where(px == 0, 0.0, jnp.where(even_x, xb_ref[...], xa_ref[...]).astype(f32))
    high = jnp.where(px == gx - 1, 0.0, jnp.where(even_x, xa_ref[...], xb_ref[...]).astype(f32))
    lane = lax.broadcasted_iota(jnp.int32, (by, bz), 1)
    planes = []
    for i, (x, before, after) in enumerate(((0, low, f_ref[1].astype(f32)), (bx - 1, f_ref[bx - 2].astype(f32), high))):
        grad = (after - before, edge[2 * i], along_lanes(f_ref[x].astype(f32), lane))
        planes.append(([grad[c] * grad[d] for c, d in PAIRS], [grad[c] * edge[2 * i + 1] for c in range(3)]))
    w = w_ref[...]
    along_y = []
    for c in range(3):
        tiles = []
        for ix in range(3):
            tile = moment[:, (c * 3 + ix) * bz : (c * 3 + ix + 1) * bz]
            pieces = []
            for s in range(2):
                first, last = planes[0][0][s * 3 + c], planes[1][0][s * 3 + c]
                same, cross = tile[s * 64 : s * 64 + 32], tile[s * 64 + 32 : s * 64 + 64]
                if ix == 0:
                    same = same + first
                elif ix == 1:
                    same, cross = same + last * (1 / 256), cross + last * (15 / 256)
                else:
                    same = same + last * (225 / 256)
                pieces += [same, cross]
            first, last = planes[0][1][c], planes[1][1][c]
            pieces.append(tile[128:160] + (first, last * (1 / 16), last * (15 / 16))[ix])
            tiles.append(jnp.concatenate(pieces, axis=0))
        sums = 0.0
        for part in split3(jnp.concatenate(tiles, axis=1)):
            sums = sums + jnp.dot(w, part, preferred_element_type=f32)
        along_y.append(sums)
    stacked = jnp.concatenate(
        [along_y[c][(24 if ix == 2 else 0) : (48 if ix == 2 else 24), ix * bz : (ix + 1) * bz] for c in range(3) for ix in range(3)],
        axis=0,
    )
    z = z_ref[...]
    along_z = 0.0
    for part in split3(stacked):
        along_z = along_z + jnp.dot(part, z, preferred_element_type=f32)

    slot = lax.broadcasted_iota(jnp.int32, (8, bz), 1) // NZN
    row = lax.broadcasted_iota(jnp.int32, (8, bz), 0)
    rows_out = [jnp.zeros((8, bz), f32) for _ in range(3)]

    def place(group_at, value, src, dst, mask=None):
        shift = ((dst - src) * NZN) % bz
        moved = pltpu.roll(value, shift, 1) if shift else value
        keep = slot == dst
        if mask is not None:
            keep = keep & mask
        rows_out[group_at] = jnp.where(keep, moved, rows_out[group_at])

    for c in range(3):
        for ix in range(2):
            at = (c * 3 + ix) * 24
            base = c * 4 + ix * 2
            v0, v1, v2 = (along_z[at + i * 8 : at + i * 8 + 8] for i in range(3))
            for tz in range(2):
                place(tz, v0, tz, base)
                place(tz, v1, tz, base + 1)
                place(2, v2, tz, base + tz, row < 4)
            place(2, v2, 2, base, (row >= 4) & (row < 7))
        at = (c * 3 + 2) * 24
        v0, v1, v2 = (along_z[at + i * 8 : at + i * 8 + 8] for i in range(3))
        for tz in range(2):
            place(c, v0, tz, 12 + tz, (row < 4) if c == 2 else None)
            place(2, v1, tz, c * 4 + tz, row == 7)
            place(2, v2, tz, c * 4 + 2 + tz, row == 7)
        place(2, v1, 2, c * 4 + 1, (row >= 4) & (row < 7))
        if c == 2:
            for tz in range(2):
                place(2, v0, tz, 12 + tz, row >= 4)
    for i in range(3):
        for copy in range(out_ref.shape[0]):
            out_ref[copy, i * 8 : i * 8 + 8, :] = rows_out[i]


def solve_kernel(gx, gy, mine_ref, other_ref, up_ref, res_ref, table, vectors):
    count, half, step = gx * gy, gx * gy // 2, gy // 2
    px, qy = lax.axis_index("gx"), lax.axis_index("gy")
    odd = lax.rem(qy, 2)
    f32 = jnp.float32
    shape = (count, 128)
    lane = lax.broadcasted_iota(jnp.int32, shape, 1)
    device = lax.broadcasted_iota(jnp.int32, shape, 0)
    core = device >= half
    place = jnp.where(core, device - half, device)
    chip = lax.rem(place, step)
    slot = lane // NZN
    own = lane < OWN
    ix1 = lax.rem(slot, 4) >= 2
    iy1 = lax.rem(slot, 2) == 1
    corner = own & (lax.rem(slot, 4) == 0)
    y_low = own & ~iy1
    first_p, last_p = place < step, place >= half - step
    first_q, last_q = (chip == 0) & ~core, (chip == step - 1) & core
    is_odd = jnp.full((half, 128), odd, jnp.int32) == 1

    def row(r):
        a, b = mine_ref[pl.ds(r, half, stride=24), :], other_ref[pl.ds(r, half, stride=24), :]
        return jnp.concatenate([jnp.where(is_odd, b, a), jnp.where(is_odd, a, b)], axis=0)

    rows = [row(r) for r in range(24)]

    def lanes(value, shift):
        shift = shift % 128
        return pltpu.roll(value, shift, 1) if shift else value

    def down(value, shift):
        shift = shift % value.shape[0]
        return pltpu.roll(value, shift, 0) if shift else value

    def next_x(value, sign):
        return down(value, -sign * step)

    def next_y(value, sign):
        low, high = value[:half], value[half:]
        if sign > 0:
            return jnp.concatenate([high, down(low, -1)], axis=0)
        return jnp.concatenate([down(high, 1), low], axis=0)

    def from_below_x(value):
        return jnp.where(first_p, 0.0, next_x(value, -1))

    def from_below_y(value):
        return jnp.where(first_q, 0.0, next_y(value, -1))

    def slots(value, src, dst):
        return lanes(value, (dst - src) * NZN)

    def xp(v):
        return jnp.where(ix1, next_x(lanes(v, 18), 1), lanes(v, -18))

    def xm(v):
        return jnp.where(ix1, lanes(v, 18), next_x(lanes(v, -18), -1))

    def yp(v):
        return jnp.where(iy1, next_y(lanes(v, 9), 1), lanes(v, -9))

    def ym(v):
        return jnp.where(iy1, lanes(v, 9), next_y(lanes(v, -9), -1))

    def turn(v, j):
        if j == 1:
            return jnp.where(lane < 72, lanes(v, -36), lanes(v, 72))
        return jnp.where(lane < 36, lanes(v, -72), lanes(v, 36))

    for s in range(2):
        for tx in range(2):
            for ty in range(2):
                for tz in range(2):
                    entry = jnp.where(own, rows[tz * 8 + s * 4 + tx * 2 + ty], 0.0)
                    if ty == 0:
                        spill = slots(rows[16 + s * 2 + tx], tz, 0)
                        entry = entry + from_below_y(jnp.where(y_low, spill, 0.0))
                    if tx == 0:
                        spill = jnp.zeros(shape, f32)
                        for c in range(3):
                            for iy in range(2):
                                moved = slots(rows[c * 8 + iy * 4 + s * 2 + ty], 12 + tz, c * 4 + iy)
                                spill = jnp.where(slot == c * 4 + iy, moved, spill)
                        if ty == 0:
                            both = slots(rows[23], s * 2 + tz, 0)
                            spill = spill + from_below_y(jnp.where(corner, both, 0.0))
                        entry = entry + from_below_x(spill)
                    if tx == 1:
                        entry = jnp.where(last_p & ix1, 0.0, entry)
                    if ty == 1:
                        entry = jnp.where(last_q & iy1, 0.0, entry)
                    kind = tx * 4 + ty * 2 + tz
                    if s == 0:
                        table[kind] = entry
                    else:
                        table[8 + kind] = jnp.where(own, turn(entry, 2), 0.0)
                        table[16 + kind] = entry

    r0, r1, r2 = rows[20], rows[21], rows[22]
    rhs = jnp.where(iy1, lanes(r1, 9), r0) + from_below_y(jnp.where(iy1, 0.0, r2))
    far = jnp.where(iy1, r1, lanes(r0, -9)) + from_below_y(jnp.where(iy1, 0.0, lanes(r2, -9)))
    rhs = rhs + from_below_x(jnp.where(ix1, 0.0, far))
    rhs = jnp.where(own, rhs, 0.0)

    def operate(v):
        upper = [v, lanes(v, -1)]
        upper += [yp(u) for u in upper]
        upper += [xp(u) for u in upper]
        parts = []
        for s in range(3):
            low = []
            for to in range(8):
                found = 0.0
                for up in range(8):
                    if up & to == 0:
                        found = found + table[8 * s + (up | to)] * upper[up]
                low.append(found)
            by_z = [low[2 * i] + lanes(low[2 * i + 1], 1) for i in range(4)]
            by_y = [by_z[2 * i] + ym(by_z[2 * i + 1]) for i in range(2)]
            parts.append(by_y[0] + xm(by_y[1]))
        coupled = parts[0] + turn(parts[1], 1) + turn(parts[2], 2)
        return damping * v + jnp.where(own, coupled, 0.0)

    def total(v):
        return jnp.sum(jnp.sum(v, axis=0, keepdims=True), axis=1, keepdims=True)

    def iterate(_, state):
        update, residual, direction, norm_now = state
        image = operate(direction)
        alpha = norm_now / total(direction * image)
        update = update + alpha * direction
        residual = residual - alpha * image
        norm_next = total(residual * residual)
        direction = residual + (norm_next / norm_now) * direction
        return update, residual, direction, norm_next

    start = (jnp.zeros(shape, f32), rhs, rhs, total(rhs * rhs))
    for turn_at in range(ITERS):
        start = iterate(turn_at, start)
    update, residual, _, _ = start
    vectors[0] = update
    vectors[1] = residual
    me = odd * half + px * step + qy // 2
    for i, ref in enumerate((up_ref, res_ref)):
        line = vectors[i, pl.ds(me, 1), :]
        for c in range(3):
            for ix in range(2):
                for iy in range(2):
                    ref[c, ix, iy : iy + 1, :] = lanes(line, -(c * 4 + ix * 2 + iy) * NZN)[:, :NZN]


LIMIT = 24 * 2**20
VMEM = pl.BlockSpec(memory_space=pltpu.VMEM)
SMEM = pl.BlockSpec(memory_space=pltpu.SMEM)


def exchange(value, gx, gy, axis, start):
    def partner(p, q):
        at, count = (p, gx) if axis == "gx" else (q, gy)
        other = at + 1 if (at - start) % 2 == 0 else at - 1
        if 0 <= other < count:
            return (other, q) if axis == "gx" else (p, other)
        return (p, q ^ 1) if axis == "gx" else (p ^ 1, q)

    pairs = []
    for p in range(gx):
        for q in range(gy):
            to = partner(p, q)
            pairs.append((p * gy + q, to[0] * gy + to[1]))
    return lax.ppermute(value, ("gx", "gy"), pairs)


def local(reference_scan, deformed_scan, source_column):
    bx, by, bz = reference_scan.shape
    gx, gy = lax.axis_size("gx"), lax.axis_size("gy")
    half = jnp.bfloat16
    rb = exchange(deformed_scan, gx, gy, "gy", 1)
    ra = exchange(deformed_scan, gx, gy, "gy", 0)
    ya, yb, xa, xb = pl.pallas_call(
        pack_kernel,
        out_shape=[jax.ShapeDtypeStruct((bx, bz), half)] * 2 + [jax.ShapeDtypeStruct((by, bz), half)] * 2,
        in_specs=[VMEM],
        out_specs=[VMEM] * 4,
        compiler_params=pltpu.CompilerParams(vmem_limit_bytes=LIMIT),
        name="pack",
    )(reference_scan)
    ya = exchange(ya, gx, gy, "gy", 0)
    xb = exchange(xb, gx, gy, "gx", 1)
    xa = exchange(xa, gx, gy, "gx", 0)
    yb = exchange(yb, gx, gy, "gy", 1)
    moment, edge = pl.pallas_call(
        functools.partial(interior_kernel, gy),
        out_shape=[jax.ShapeDtypeStruct((160, 9 * bz), jnp.float32), jax.ShapeDtypeStruct((4, by, bz), jnp.float32)],
        in_specs=[VMEM] * 6 + [SMEM],
        out_specs=[VMEM] * 2,
        scratch_shapes=[
            pltpu.VMEM((bx, by + 16, bz), jnp.float32),
            pltpu.VMEM((bx, by, bz), jnp.float32),
            pltpu.VMEM((bx, by, bz), jnp.float32),
            pltpu.VMEM((bx // 8, by, bz), jnp.int32),
        ],
        compiler_params=pltpu.CompilerParams(vmem_limit_bytes=LIMIT),
        cost_estimate=pl.CostEstimate(flops=8_000_000, bytes_accessed=2_000_000, transcendentals=0),
        name="interior",
    )(reference_scan, deformed_scan, ra, rb, ya, yb, source_column[0, :, :, 0])
    w, z = weights()
    payload = pl.pallas_call(
        functools.partial(finish_kernel, gx),
        out_shape=jax.ShapeDtypeStruct((gx * gy // 2, 24, bz), jnp.float32),
        in_specs=[VMEM] * 7,
        out_specs=VMEM,
        compiler_params=pltpu.CompilerParams(vmem_limit_bytes=LIMIT),
        name="finish",
    )(reference_scan, xa, xb, edge, moment, jnp.asarray(w, half), jnp.asarray(z, half))
    groups = [[i * 2 + core for i in range(gx * gy // 2)] for core in range(2)]
    mine = lax.all_to_all(payload, ("gx", "gy"), 0, 0, axis_index_groups=groups)
    other = lax.ppermute(mine, "gy", [(i, i ^ 1) for i in range(gy)])
    out = jax.ShapeDtypeStruct((3, 2, 2, NZN), jnp.float32)
    update, residual = pl.pallas_call(
        functools.partial(solve_kernel, gx, gy),
        out_shape=[out, out],
        in_specs=[VMEM] * 2,
        out_specs=[VMEM] * 2,
        scratch_shapes=[
            pltpu.VMEM((24, gx * gy, bz), jnp.float32),
            pltpu.VMEM((2, gx * gy, bz), jnp.float32),
        ],
        compiler_params=pltpu.CompilerParams(vmem_limit_bytes=LIMIT),
        name="solve",
    )(mine.reshape(-1, bz), other.reshape(-1, bz))
    return update, residual


def solution(mesh):
    return jax.shard_map(
        local,
        mesh=mesh,
        in_specs=(P("gx", "gy", None), P("gx", "gy", None), P("gx", None, None, None)),
        out_specs=(P(None, "gx", "gy", None), P(None, "gx", "gy", None)),
        check_vma=False,
    )
```

```python
import functools

import jax
import jax.numpy as jnp
import numpy as np
from jax import lax
from jax.experimental import pallas as pl
from jax.experimental.pallas import tpu as pltpu
from jax.sharding import PartitionSpec as P

E = 16
ITERS = 4
NZN = 9
CAP = 16
BLOCKS = 64
CHUNKS = 8
OWN = 12 * NZN


damping = 0.1


def weights():
    m = np.arange(E, 0, -1, dtype=np.float64) / E
    same_low, cross, same_high, low, high = m * m, m * (1 - m), (1 - m) ** 2, m, 1 - m

    def along(count):
        d = np.zeros((count + 1, count * E))
        o = np.zeros((count + 1, count * E))
        h = np.zeros((count + 1, count * E))
        for e in range(count):
            at = slice(e * E, (e + 1) * E)
            d[e, at] += same_low
            d[e + 1, at] += same_high
            o[e, at] += cross
            h[e, at] += low
            h[e + 1, at] += high
        return d, o, h

    yd, yo, yh = along(2)
    w = np.zeros((48, 160))
    for s in range(2):
        for tx in range(2):
            k = slice((s * 2 + tx) * 32, (s * 2 + tx) * 32 + 32)
            for iy in range(2):
                w[iy * 8 + s * 4 + tx * 2 + 0, k] = yd[iy]
                w[iy * 8 + s * 4 + tx * 2 + 1, k] = yo[iy]
            w[16 + s * 2 + tx, k] = yd[2]
        k = slice(s * 64, s * 64 + 32)
        for iy in range(2):
            w[24 + iy * 4 + s * 2 + 0, k] = yd[iy]
            w[24 + iy * 4 + s * 2 + 1, k] = yo[iy]
        w[(32 if s == 0 else 40) + 7, k] = yd[2]
    for iy in range(3):
        w[20 + iy, 128:160] = yh[iy]
        w[32 + 4 + iy, 128:160] = yh[iy]
    zd, zo, zh = along(8)
    z = np.zeros((128, 128))
    scale = 1.0 / (2.0 * E)
    z[:, 0:9] = zd.T * scale * scale
    z[:, 9:18] = zo.T * scale * scale
    z[:, 18:27] = zh.T * scale
    return w.astype(np.float32), z.astype(np.float32)


def split3(value):
    high = value.astype(jnp.bfloat16)
    rest = value - high.astype(jnp.float32)
    mid = rest.astype(jnp.bfloat16)
    low = (rest - mid.astype(jnp.float32)).astype(jnp.bfloat16)
    return high, mid, low


def neighbours(q, gy):
    even = lax.rem(q, 2) == 0
    return jnp.where(even, q + 1, q - 1), jnp.where(even, q - 1, q + 1)


def block_lists(table, q, gy):
    first, second = neighbours(q, gy)
    own = table[pl.ds(q, 1), :]
    match = [table[pl.ds(jnp.clip(to, 0, gy - 1), 1), :] == q for to in (first, second)] + [own == to for to in (first, second)]
    match = jnp.concatenate([m.astype(jnp.float32) for m in match] * 2, axis=0).astype(jnp.bfloat16)
    row = lax.broadcasted_iota(jnp.int32, (BLOCKS, BLOCKS), 0)
    col = lax.broadcasted_iota(jnp.int32, (BLOCKS, BLOCKS), 1)

    def against(matrix):
        matrix = matrix.astype(jnp.float32).astype(jnp.bfloat16)
        return lax.dot_general(matrix, match, (((1,), (1,)), ((), ())), preferred_element_type=jnp.float32)

    rank, taken = against(col < row), against(col == row)
    slot = lax.broadcasted_iota(jnp.int32, (BLOCKS, 128), 1).astype(jnp.float32)
    number = (lax.broadcasted_iota(jnp.int32, (BLOCKS, 128), 0) + 1).astype(jnp.float32)
    rows = []
    for i in range(4):
        here = (rank[:, i : i + 1] == slot) & (taken[:, i : i + 1] > 0.5)
        rows.append(jnp.sum(jnp.where(here, number, 0.0), axis=0, keepdims=True))
    return (jnp.concatenate(rows * 2, axis=0) - 1.0).astype(jnp.int32)


def pack_kernel(gy, f_hbm, d_hbm, col_hbm, ya_ref, yb_ref, xa_ref, xb_ref, f_ref, d_ref, lists, col_ref, list_ref, sems, sem):
    even_x = lax.rem(lax.axis_index("gx"), 2) == 0
    q = lax.axis_index("gy")
    even_y = lax.rem(q, 2) == 0
    bx, groups, sub, bz = f_hbm.shape
    chunk = bx // CHUNKS
    fetch = pltpu.make_async_copy(col_hbm, col_ref, sem.at[0])
    fetch.start()
    copies = []
    for n, (src, dst) in enumerate(((d_hbm, d_ref), (f_hbm, f_ref))):
        for i in range(CHUNKS):
            at = pl.ds(i * chunk, chunk)
            copies.append(pltpu.make_async_copy(src.at[at], dst.at[at], sems.at[n, i]))
            copies[-1].start()
    fetch.wait()
    lists[...] = block_lists(col_ref, q, gy)
    move = pltpu.make_async_copy(lists, list_ref, sem.at[1])
    move.start()
    move.wait()
    for copy in copies:
        copy.wait()
    quarter = lax.broadcasted_iota(jnp.int32, (64, bz), 1) // (bz // 4)
    for n, ref in enumerate((ya_ref, yb_ref)):
        for tile in range(CAP // 4):
            held = jnp.zeros((64, bz), jnp.float32)
            for k in range(4):
                block = jnp.maximum(list_ref[n, tile * 4 + k], 0)
                piece = d_ref[pl.ds((block >> 4) * 8, 8), (block >> 2) & 3].astype(jnp.float32).reshape(64, bz)
                turned = pltpu.roll(piece, ((k - block) & 3) * (bz // 4), 1)
                held = jnp.where(quarter == k, turned, held)
            ref[tile * 8 : tile * 8 + 8] = held.astype(jnp.bfloat16).reshape(8, sub, bz)
    head, tail = f_ref[:, 0, 0, :], f_ref[:, groups - 1, sub - 1, :]
    ya_ref[CAP * 2 :] = jnp.where(even_y, tail, head).reshape(bx // sub, sub, bz)
    yb_ref[CAP * 2 :] = jnp.where(even_y, head, tail).reshape(bx // sub, sub, bz)
    first, last = f_ref[0], f_ref[bx - 1]
    xa_ref[...] = jnp.where(even_x, last, first)
    xb_ref[...] = jnp.where(even_x, first, last)


PAIRS = ((0, 0), (1, 1), (2, 2), (0, 1), (1, 2), (2, 0))


def along_lanes(now, lane):
    size = now.shape[-1]
    up = jnp.where(lane == size - 1, 0.0, pltpu.roll(now, size - 1, 1))
    return up - jnp.where(lane == 0, 0.0, pltpu.roll(now, 1, 1))


def interior_kernel(gy, f_ref, d_ref, ra_ref, rb_ref, list_ref, moment, edge, field, slope, misfit):
    qy = lax.axis_index("gy")
    even_y = lax.rem(qy, 2) == 0
    bx, by, bz = f_ref.shape
    f32 = jnp.float32
    lane = lax.broadcasted_iota(jnp.int32, (8, bz), 1)
    rim_a, rim_b = (ref[CAP * 2 :].astype(f32).reshape(bx, bz) for ref in (ra_ref, rb_ref))
    rim_low, rim_high = jnp.where(even_y, rim_b, rim_a), jnp.where(even_y, rim_a, rim_b)
    field[:, 7, :] = jnp.where(qy == 0, 0.0, rim_low)
    field[:, 8 + by, :] = jnp.where(qy == gy - 1, 0.0, rim_high)

    def prepare(x, _):
        here = f_ref[x].astype(f32)
        field[x, 8 : 8 + by, :] = here
        slope[x] = field[x, 9 : 9 + by, :] - field[x, 7 : 7 + by, :]
        misfit[x] = here - d_ref[x].astype(f32)
        return 0

    lax.fori_loop(0, bx, prepare, 0, unroll=4)
    quarter = lax.broadcasted_iota(jnp.int32, (8, 8, bz), 2) // (bz // 4)
    for n, ref in enumerate((ra_ref, rb_ref)):
        for tile in range(CAP // 4):
            held = ref[tile * 8 : tile * 8 + 8].astype(f32).reshape(64, bz)
            for k in range(4):
                listed = list_ref[2 + n, tile * 4 + k]
                block = jnp.maximum(listed, 0)
                turned = pltpu.roll(held, ((block - k) & 3) * (bz // 4), 1).reshape(8, 8, bz)
                here = quarter == jnp.where(listed < 0, -1, block & 3)
                planes = pl.ds((block >> 4) * 8, 8)
                start = ((block >> 2) & 3) * 8
                at = pl.ds(pl.multiple_of(start, 8), 8)
                at_f = pl.ds(pl.multiple_of(start + 8, 8), 8)
                misfit[planes, at, :] = jnp.where(here, field[planes, at_f, :] - turned, misfit[planes, at, :])
    for i, x in enumerate((0, bx - 1)):
        edge[2 * i] = slope[x]
        edge[2 * i + 1] = misfit[x]

    def group(g, _):
        rows = pl.ds(pl.multiple_of(g * 8, 8), 8)
        rows_f = pl.ds(pl.multiple_of(g * 8 + 8, 8), 8)
        found = []
        for e in range(2):
            first = e * E + (1 if e == 0 else 0)
            last = e * E + E - (2 if e == 1 else 1)
            before, now = field[first - 1, rows_f, :], field[first, rows_f, :]
            tot = [[jnp.zeros((8, bz), f32) for _ in range(3)] for _ in range(6)]
            right = [[jnp.zeros((8, bz), f32) for _ in range(2)] for _ in range(3)]
            for x in range(first, last + 1):
                after = field[x + 1, rows_f, :]
                grad = (after - before, slope[x, rows, :], along_lanes(now, lane))
                for n, (c, d) in enumerate(PAIRS):
                    tot[n][0] = tot[n][0] + grad[c] * grad[d]
                    tot[n][1] = tot[n][1] + tot[n][0]
                    tot[n][2] = tot[n][2] + tot[n][1]
                miss = misfit[x, rows, :]
                for c in range(3):
                    right[c][0] = right[c][0] + grad[c] * miss
                    right[c][1] = right[c][1] + right[c][0]
                before, now = now, after
            if e == 1:
                for n in range(6):
                    tot[n][1] = tot[n][1] + tot[n][0]
                    tot[n][2] = tot[n][2] + tot[n][1]
                for c in range(3):
                    right[c][1] = right[c][1] + right[c][0]
            ent = []
            for n in range(6):
                a0, a1, a2 = tot[n]
                sq = 2.0 * a2 - a1
                ent.append((sq * (1 / 256), (16.0 * a1 - sq) * (1 / 256), a0 - a1 * (1 / 8) + sq * (1 / 256)))
            rh = [(right[c][1] * (1 / 16), right[c][0] - right[c][1] * (1 / 16)) for c in range(3)]
            found.append((ent, rh))
        for s in range(2):
            for c in range(3):
                e0, e1 = found[0][0][s * 3 + c], found[1][0][s * 3 + c]
                same = (e0[0], e0[2] + e1[0], e1[2])
                cross = (e0[1], e1[1], jnp.zeros((8, bz), f32))
                for ix in range(3):
                    at = slice((c * 3 + ix) * bz, (c * 3 + ix + 1) * bz)
                    moment[pl.ds(pl.multiple_of(s * 64 + g * 8, 8), 8), at] = same[ix]
                    moment[pl.ds(pl.multiple_of(s * 64 + 32 + g * 8, 8), 8), at] = cross[ix]
        for c in range(3):
            r0, r1 = found[0][1][c], found[1][1][c]
            for ix, value in enumerate((r0[0], r0[1] + r1[0], r1[1])):
                at = slice((c * 3 + ix) * bz, (c * 3 + ix + 1) * bz)
                moment[pl.ds(pl.multiple_of(128 + g * 8, 8), 8), at] = value
        return 0

    lax.fori_loop(0, by // 8, group, 0)


def finish_kernel(gx, f_ref, xa_ref, xb_ref, edge, moment, w_ref, z_ref, out_ref):
    px = lax.axis_index("gx")
    even_x = lax.rem(px, 2) == 0
    bx, by, bz = f_ref.shape
    f32 = jnp.float32
    low = jnp.where(px == 0, 0.0, jnp.where(even_x, xb_ref[...], xa_ref[...]).astype(f32))
    high = jnp.where(px == gx - 1, 0.0, jnp.where(even_x, xa_ref[...], xb_ref[...]).astype(f32))
    lane = lax.broadcasted_iota(jnp.int32, (by, bz), 1)
    planes = []
    for i, (x, before, after) in enumerate(((0, low, f_ref[1].astype(f32)), (bx - 1, f_ref[bx - 2].astype(f32), high))):
        grad = (after - before, edge[2 * i], along_lanes(f_ref[x].astype(f32), lane))
        planes.append(([grad[c] * grad[d] for c, d in PAIRS], [grad[c] * edge[2 * i + 1] for c in range(3)]))
    w = w_ref[...]
    along_y = []
    for c in range(3):
        tiles = []
        for ix in range(3):
            tile = moment[:, (c * 3 + ix) * bz : (c * 3 + ix + 1) * bz]
            pieces = []
            for s in range(2):
                first, last = planes[0][0][s * 3 + c], planes[1][0][s * 3 + c]
                same, cross = tile[s * 64 : s * 64 + 32], tile[s * 64 + 32 : s * 64 + 64]
                if ix == 0:
                    same = same + first
                elif ix == 1:
                    same, cross = same + last * (1 / 256), cross + last * (15 / 256)
                else:
                    same = same + last * (225 / 256)
                pieces += [same, cross]
            first, last = planes[0][1][c], planes[1][1][c]
            pieces.append(tile[128:160] + (first, last * (1 / 16), last * (15 / 16))[ix])
            tiles.append(jnp.concatenate(pieces, axis=0))
        sums = 0.0
        for part in split3(jnp.concatenate(tiles, axis=1)):
            sums = sums + jnp.dot(w, part, preferred_element_type=f32)
        along_y.append(sums)
    stacked = jnp.concatenate(
        [along_y[c][(24 if ix == 2 else 0) : (48 if ix == 2 else 24), ix * bz : (ix + 1) * bz] for c in range(3) for ix in range(3)],
        axis=0,
    )
    z = z_ref[...]
    along_z = 0.0
    for part in split3(stacked):
        along_z = along_z + jnp.dot(part, z, preferred_element_type=f32)

    slot = lax.broadcasted_iota(jnp.int32, (8, bz), 1) // NZN
    row = lax.broadcasted_iota(jnp.int32, (8, bz), 0)
    rows_out = [jnp.zeros((8, bz), f32) for _ in range(3)]

    def place(group_at, value, src, dst, mask=None):
        shift = ((dst - src) * NZN) % bz
        moved = pltpu.roll(value, shift, 1) if shift else value
        keep = slot == dst
        if mask is not None:
            keep = keep & mask
        rows_out[group_at] = jnp.where(keep, moved, rows_out[group_at])

    for c in range(3):
        for ix in range(2):
            at = (c * 3 + ix) * 24
            base = c * 4 + ix * 2
            v0, v1, v2 = (along_z[at + i * 8 : at + i * 8 + 8] for i in range(3))
            for tz in range(2):
                place(tz, v0, tz, base)
                place(tz, v1, tz, base + 1)
                place(2, v2, tz, base + tz, row < 4)
            place(2, v2, 2, base, (row >= 4) & (row < 7))
        at = (c * 3 + 2) * 24
        v0, v1, v2 = (along_z[at + i * 8 : at + i * 8 + 8] for i in range(3))
        for tz in range(2):
            place(c, v0, tz, 12 + tz, (row < 4) if c == 2 else None)
            place(2, v1, tz, c * 4 + tz, row == 7)
            place(2, v2, tz, c * 4 + 2 + tz, row == 7)
        place(2, v1, 2, c * 4 + 1, (row >= 4) & (row < 7))
        if c == 2:
            for tz in range(2):
                place(2, v0, tz, 12 + tz, row >= 4)
    for i in range(3):
        for copy in range(out_ref.shape[0]):
            out_ref[copy, i * 8 : i * 8 + 8, :] = rows_out[i]


def solve_kernel(gx, gy, mine_ref, other_ref, up_ref, res_ref, table, vectors):
    count, half, step = gx * gy, gx * gy // 2, gy // 2
    px, qy = lax.axis_index("gx"), lax.axis_index("gy")
    odd = lax.rem(qy, 2)
    f32 = jnp.float32
    shape = (count, 128)
    lane = lax.broadcasted_iota(jnp.int32, shape, 1)
    device = lax.broadcasted_iota(jnp.int32, shape, 0)
    core = device >= half
    place = jnp.where(core, device - half, device)
    chip = lax.rem(place, step)
    slot = lane // NZN
    own = lane < OWN
    ix1 = lax.rem(slot, 4) >= 2
    iy1 = lax.rem(slot, 2) == 1
    corner = own & (lax.rem(slot, 4) == 0)
    y_low = own & ~iy1
    first_p, last_p = place < step, place >= half - step
    first_q, last_q = (chip == 0) & ~core, (chip == step - 1) & core
    is_odd = jnp.full((half, 128), odd, jnp.int32) == 1

    def row(r):
        a, b = mine_ref[pl.ds(r, half, stride=24), :], other_ref[pl.ds(r, half, stride=24), :]
        return jnp.concatenate([jnp.where(is_odd, b, a), jnp.where(is_odd, a, b)], axis=0)

    rows = [row(r) for r in range(24)]

    def lanes(value, shift):
        shift = shift % 128
        return pltpu.roll(value, shift, 1) if shift else value

    def down(value, shift):
        shift = shift % value.shape[0]
        return pltpu.roll(value, shift, 0) if shift else value

    def next_x(value, sign):
        return down(value, -sign * step)

    def next_y(value, sign):
        low, high = value[:half], value[half:]
        if sign > 0:
            return jnp.concatenate([high, down(low, -1)], axis=0)
        return jnp.concatenate([down(high, 1), low], axis=0)

    def from_below_x(value):
        return jnp.where(first_p, 0.0, next_x(value, -1))

    def from_below_y(value):
        return jnp.where(first_q, 0.0, next_y(value, -1))

    def slots(value, src, dst):
        return lanes(value, (dst - src) * NZN)

    def xp(v):
        return jnp.where(ix1, next_x(lanes(v, 18), 1), lanes(v, -18))

    def xm(v):
        return jnp.where(ix1, lanes(v, 18), next_x(lanes(v, -18), -1))

    def yp(v):
        return jnp.where(iy1, next_y(lanes(v, 9), 1), lanes(v, -9))

    def ym(v):
        return jnp.where(iy1, lanes(v, 9), next_y(lanes(v, -9), -1))

    def turn(v, j):
        if j == 1:
            return jnp.where(lane < 72, lanes(v, -36), lanes(v, 72))
        return jnp.where(lane < 36, lanes(v, -72), lanes(v, 36))

    for s in range(2):
        for tx in range(2):
            for ty in range(2):
                for tz in range(2):
                    entry = jnp.where(own, rows[tz * 8 + s * 4 + tx * 2 + ty], 0.0)
                    if ty == 0:
                        spill = slots(rows[16 + s * 2 + tx], tz, 0)
                        entry = entry + from_below_y(jnp.where(y_low, spill, 0.0))
                    if tx == 0:
                        spill = jnp.zeros(shape, f32)
                        for c in range(3):
                            for iy in range(2):
                                moved = slots(rows[c * 8 + iy * 4 + s * 2 + ty], 12 + tz, c * 4 + iy)
                                spill = jnp.where(slot == c * 4 + iy, moved, spill)
                        if ty == 0:
                            both = slots(rows[23], s * 2 + tz, 0)
                            spill = spill + from_below_y(jnp.where(corner, both, 0.0))
                        entry = entry + from_below_x(spill)
                    if tx == 1:
                        entry = jnp.where(last_p & ix1, 0.0, entry)
                    if ty == 1:
                        entry = jnp.where(last_q & iy1, 0.0, entry)
                    kind = tx * 4 + ty * 2 + tz
                    if s == 0:
                        table[kind] = entry
                    else:
                        table[8 + kind] = jnp.where(own, turn(entry, 2), 0.0)
                        table[16 + kind] = entry

    r0, r1, r2 = rows[20], rows[21], rows[22]
    rhs = jnp.where(iy1, lanes(r1, 9), r0) + from_below_y(jnp.where(iy1, 0.0, r2))
    far = jnp.where(iy1, r1, lanes(r0, -9)) + from_below_y(jnp.where(iy1, 0.0, lanes(r2, -9)))
    rhs = rhs + from_below_x(jnp.where(ix1, 0.0, far))
    rhs = jnp.where(own, rhs, 0.0)

    def operate(v):
        upper = [v, lanes(v, -1)]
        upper += [yp(u) for u in upper]
        upper += [xp(u) for u in upper]
        parts = []
        for s in range(3):
            low = []
            for to in range(8):
                found = 0.0
                for up in range(8):
                    if up & to == 0:
                        found = found + table[8 * s + (up | to)] * upper[up]
                low.append(found)
            by_z = [low[2 * i] + lanes(low[2 * i + 1], 1) for i in range(4)]
            by_y = [by_z[2 * i] + ym(by_z[2 * i + 1]) for i in range(2)]
            parts.append(by_y[0] + xm(by_y[1]))
        coupled = parts[0] + turn(parts[1], 1) + turn(parts[2], 2)
        return damping * v + jnp.where(own, coupled, 0.0)

    def total(v):
        return jnp.sum(jnp.sum(v, axis=0, keepdims=True), axis=1, keepdims=True)

    def iterate(_, state):
        update, residual, direction, norm_now = state
        image = operate(direction)
        alpha = norm_now / total(direction * image)
        update = update + alpha * direction
        residual = residual - alpha * image
        norm_next = total(residual * residual)
        direction = residual + (norm_next / norm_now) * direction
        return update, residual, direction, norm_next

    start = (jnp.zeros(shape, f32), rhs, rhs, total(rhs * rhs))
    for turn_at in range(ITERS):
        start = iterate(turn_at, start)
    update, residual, _, _ = start
    vectors[0] = update
    vectors[1] = residual
    me = odd * half + px * step + qy // 2
    for i, ref in enumerate((up_ref, res_ref)):
        line = vectors[i, pl.ds(me, 1), :]
        for c in range(3):
            for ix in range(2):
                for iy in range(2):
                    ref[c, ix, iy : iy + 1, :] = lanes(line, -(c * 4 + ix * 2 + iy) * NZN)[:, :NZN]


LIMIT = 24 * 2**20
PACK_LIMIT = 55_750_000
HBM = pl.BlockSpec(memory_space=pltpu.MemorySpace.HBM)
VMEM = pl.BlockSpec(memory_space=pltpu.VMEM)
SMEM = pl.BlockSpec(memory_space=pltpu.SMEM)


def exchange(value, gx, gy, axis, start):
    def partner(p, q):
        at, count = (p, gx) if axis == "gx" else (q, gy)
        other = at + 1 if (at - start) % 2 == 0 else at - 1
        if 0 <= other < count:
            return (other, q) if axis == "gx" else (p, other)
        return (p, q ^ 1) if axis == "gx" else (p ^ 1, q)

    pairs = []
    for p in range(gx):
        for q in range(gy):
            to = partner(p, q)
            pairs.append((p * gy + q, to[0] * gy + to[1]))
    return lax.ppermute(value, ("gx", "gy"), pairs)


def local(reference_scan, deformed_scan, source_column):
    bx, by, bz = reference_scan.shape
    gx, gy = lax.axis_size("gx"), lax.axis_size("gy")
    half = jnp.bfloat16
    table = source_column[0, :, :, 0]
    sub = 8
    split = (bx, by // sub, sub, bz)
    packed = jax.ShapeDtypeStruct((CAP * 2 + bx // sub, sub, bz), half)
    plane = jax.ShapeDtypeStruct((by // sub, sub, bz), half)
    whole = jax.ShapeDtypeStruct(split, half)
    ya, yb, xa, xb, near, moving, lists = pl.pallas_call(
        functools.partial(pack_kernel, gy),
        out_shape=[packed, packed, plane, plane, whole, whole, jax.ShapeDtypeStruct((8, 128), jnp.int32)],
        in_specs=[HBM] * 3,
        out_specs=[VMEM] * 7,
        scratch_shapes=[
            pltpu.VMEM(table.shape, jnp.int32),
            pltpu.SMEM((8, 128), jnp.int32),
            pltpu.SemaphoreType.DMA((2, CHUNKS)),
            pltpu.SemaphoreType.DMA((2,)),
        ],
        compiler_params=pltpu.CompilerParams(vmem_limit_bytes=PACK_LIMIT),
        name="pack",
    )(reference_scan.reshape(split), deformed_scan.reshape(split), table)
    rb = exchange(yb, gx, gy, "gy", 1)
    ra = exchange(ya, gx, gy, "gy", 0)
    xb = exchange(xb, gx, gy, "gx", 1).reshape(by, bz)
    xa = exchange(xa, gx, gy, "gx", 0).reshape(by, bz)
    near, moving = near.reshape(bx, by, bz), moving.reshape(bx, by, bz)
    moment, edge = pl.pallas_call(
        functools.partial(interior_kernel, gy),
        out_shape=[jax.ShapeDtypeStruct((160, 9 * bz), jnp.float32), jax.ShapeDtypeStruct((4, by, bz), jnp.float32)],
        in_specs=[VMEM] * 4 + [SMEM],
        out_specs=[VMEM] * 2,
        scratch_shapes=[
            pltpu.VMEM((bx, by + 16, bz), jnp.float32),
            pltpu.VMEM((bx, by, bz), jnp.float32),
            pltpu.VMEM((bx, by, bz), jnp.float32),
        ],
        compiler_params=pltpu.CompilerParams(vmem_limit_bytes=LIMIT),
        cost_estimate=pl.CostEstimate(flops=8_000_000, bytes_accessed=2_000_000, transcendentals=0),
        name="interior",
    )(near, moving, ra, rb, lists)
    w, z = weights()
    payload = pl.pallas_call(
        functools.partial(finish_kernel, gx),
        out_shape=jax.ShapeDtypeStruct((gx * gy // 2, 24, bz), jnp.float32),
        in_specs=[VMEM] * 7,
        out_specs=VMEM,
        compiler_params=pltpu.CompilerParams(vmem_limit_bytes=LIMIT),
        name="finish",
    )(near, xa, xb, edge, moment, jnp.asarray(w, half), jnp.asarray(z, half))
    groups = [[i * 2 + core for i in range(gx * gy // 2)] for core in range(2)]
    mine = lax.all_to_all(payload, ("gx", "gy"), 0, 0, axis_index_groups=groups)
    other = lax.ppermute(mine, "gy", [(i, i ^ 1) for i in range(gy)])
    out = jax.ShapeDtypeStruct((3, 2, 2, NZN), jnp.float32)
    update, residual = pl.pallas_call(
        functools.partial(solve_kernel, gx, gy),
        out_shape=[out, out],
        in_specs=[VMEM] * 2,
        out_specs=[VMEM] * 2,
        scratch_shapes=[
            pltpu.VMEM((24, gx * gy, bz), jnp.float32),
            pltpu.VMEM((2, gx * gy, bz), jnp.float32),
        ],
        compiler_params=pltpu.CompilerParams(vmem_limit_bytes=LIMIT),
        name="solve",
    )(mine.reshape(-1, bz), other.reshape(-1, bz))
    return update, residual


def solution(mesh):
    return jax.shard_map(
        local,
        mesh=mesh,
        in_specs=(P("gx", "gy", None), P("gx", "gy", None), P("gx", None, None, None)),
        out_specs=(P(None, "gx", "gy", None), P(None, "gx", "gy", None)),
        check_vma=False,
    )
```

```python
import functools

import jax
import jax.numpy as jnp
import numpy as np
from jax import lax
from jax.experimental import pallas as pl
from jax.experimental.pallas import tpu as pltpu
from jax.sharding import PartitionSpec as P


E = 16
ITERS = 4
NZN = 9
CAP = 16
BLOCKS = 64
CHUNKS = 2
OWN = 12 * NZN


damping = 0.1


def weights():
    m = np.arange(E, 0, -1, dtype=np.float64) / E
    same_low, cross, same_high, low, high = m * m, m * (1 - m), (1 - m) ** 2, m, 1 - m

    def along(count):
        d = np.zeros((count + 1, count * E))
        o = np.zeros((count + 1, count * E))
        h = np.zeros((count + 1, count * E))
        for e in range(count):
            at = slice(e * E, (e + 1) * E)
            d[e, at] += same_low
            d[e + 1, at] += same_high
            o[e, at] += cross
            h[e, at] += low
            h[e + 1, at] += high
        return d, o, h

    yd, yo, yh = along(2)
    w = np.zeros((48, 160))
    for s in range(2):
        for tx in range(2):
            k = slice((s * 2 + tx) * 32, (s * 2 + tx) * 32 + 32)
            for iy in range(2):
                w[iy * 8 + s * 4 + tx * 2 + 0, k] = yd[iy]
                w[iy * 8 + s * 4 + tx * 2 + 1, k] = yo[iy]
            w[16 + s * 2 + tx, k] = yd[2]
        k = slice(s * 64, s * 64 + 32)
        for iy in range(2):
            w[24 + iy * 4 + s * 2 + 0, k] = yd[iy]
            w[24 + iy * 4 + s * 2 + 1, k] = yo[iy]
        w[(32 if s == 0 else 40) + 7, k] = yd[2]
    for iy in range(3):
        w[20 + iy, 128:160] = yh[iy]
        w[32 + 4 + iy, 128:160] = yh[iy]
    zd, zo, zh = along(8)
    z = np.zeros((128, 128))
    scale = 1.0 / (2.0 * E)
    z[:, 0:9] = zd.T * scale * scale
    z[:, 9:18] = zo.T * scale * scale
    z[:, 18:27] = zh.T * scale
    return w.astype(np.float32), z.astype(np.float32)


def split3(value):
    high = value.astype(jnp.bfloat16)
    rest = value - high.astype(jnp.float32)
    mid = rest.astype(jnp.bfloat16)
    low = (rest - mid.astype(jnp.float32)).astype(jnp.bfloat16)
    return high, mid, low


def neighbours(q):
    even = lax.rem(q, 2) == 0
    return jnp.where(even, q + 1, q - 1), jnp.where(even, q - 1, q + 1)


def block_lists(table, q, gy):
    first, second = neighbours(q)
    own = table[pl.ds(q, 1), :]
    match = [table[pl.ds(jnp.clip(to, 0, gy - 1), 1), :] == q for to in (first, second)] + [own == to for to in (first, second)]
    match = jnp.concatenate([m.astype(jnp.float32) for m in match] * 2, axis=0).astype(jnp.bfloat16)
    row = lax.broadcasted_iota(jnp.int32, (BLOCKS, BLOCKS), 0)
    col = lax.broadcasted_iota(jnp.int32, (BLOCKS, BLOCKS), 1)

    def against(matrix):
        matrix = matrix.astype(jnp.float32).astype(jnp.bfloat16)
        return lax.dot_general(matrix, match, (((1,), (1,)), ((), ())), preferred_element_type=jnp.float32)

    rank, taken = against(col < row), against(col == row)
    slot = lax.broadcasted_iota(jnp.int32, (BLOCKS, 128), 1).astype(jnp.float32)
    number = (lax.broadcasted_iota(jnp.int32, (BLOCKS, 128), 0) + 1).astype(jnp.float32)
    rows = []
    for i in range(4):
        here = (rank[:, i : i + 1] == slot) & (taken[:, i : i + 1] > 0.5)
        rows.append(jnp.sum(jnp.where(here, number, 0.0), axis=0, keepdims=True))
    return (jnp.concatenate(rows * 2, axis=0) - 1.0).astype(jnp.int32)


def pack_kernel(gy, f_hbm, d_hbm, col_hbm, ya_ref, yb_ref, xa_ref, xb_ref, f_ref, d_ref, lists, col_ref, sems, sem):
    even_x = lax.rem(lax.axis_index("gx"), 2) == 0
    q = lax.axis_index("gy")
    even_y = lax.rem(q, 2) == 0
    bx, groups, sub, bz = f_hbm.shape
    chunk = bx // CHUNKS
    fetch = pltpu.make_async_copy(col_hbm, col_ref, sem)
    fetch.start()
    copies = []
    for n, (src, dst) in enumerate(((d_hbm, d_ref), (f_hbm, f_ref))):
        for i in range(CHUNKS):
            at = pl.ds(i * chunk, chunk)
            copies.append(pltpu.make_async_copy(src.at[at], dst.at[at], sems.at[n, i]))
    for copy in copies[:CHUNKS]:
        copy.start()
    fetch.wait()
    found = block_lists(col_ref, q, gy)
    lists[...] = found
    for copy in copies[CHUNKS:]:
        copy.start()
    for copy in copies[:CHUNKS]:
        copy.wait()
    quarter = lax.broadcasted_iota(jnp.int32, (64, bz), 1) // (bz // 4)
    for n, ref in enumerate((ya_ref, yb_ref)):
        for tile in range(CAP // 4):
            held = jnp.zeros((64, bz), jnp.float32)
            for k in range(4):
                block = jnp.maximum(found[n, tile * 4 + k], 0)
                piece = d_ref[pl.ds((block >> 4) * 8, 8), (block >> 2) & 3].astype(jnp.float32).reshape(64, bz)
                turned = pltpu.roll(piece, ((k - block) & 3) * (bz // 4), 1)
                held = jnp.where(quarter == k, turned, held)
            ref[tile * 8 : tile * 8 + 8] = held.astype(jnp.bfloat16).reshape(8, sub, bz)
    for copy in copies[CHUNKS:]:
        copy.wait()
    head, tail = f_ref[:, 0, 0, :], f_ref[:, groups - 1, sub - 1, :]
    ya_ref[CAP * 2 :] = jnp.where(even_y, tail, head).reshape(bx // sub, sub, bz)
    yb_ref[CAP * 2 :] = jnp.where(even_y, head, tail).reshape(bx // sub, sub, bz)
    first, last = f_ref[0], f_ref[bx - 1]
    xa_ref[...] = jnp.where(even_x, last, first)
    xb_ref[...] = jnp.where(even_x, first, last)


PAIRS = ((0, 0), (1, 1), (2, 2), (0, 1), (1, 2), (2, 0))


def along_lanes(now, lane):
    size = now.shape[-1]
    up = jnp.where(lane == size - 1, 0.0, pltpu.roll(now, size - 1, 1))
    return up - jnp.where(lane == 0, 0.0, pltpu.roll(now, 1, 1))


def interior_kernel(gy, f_ref, d_ref, ra_ref, rb_ref, lists, moment, edge, field, slope, misfit, list_ref, sem):
    move = pltpu.make_async_copy(lists, list_ref, sem)
    move.start()
    qy = lax.axis_index("gy")
    even_y = lax.rem(qy, 2) == 0
    bx, by, bz = f_ref.shape
    f32 = jnp.float32
    lane = lax.broadcasted_iota(jnp.int32, (8, bz), 1)
    rim_a, rim_b = (ref[CAP * 2 :].astype(f32).reshape(bx, bz) for ref in (ra_ref, rb_ref))
    rim_low, rim_high = jnp.where(even_y, rim_b, rim_a), jnp.where(even_y, rim_a, rim_b)
    field[:, 7, :] = jnp.where(qy == 0, 0.0, rim_low)
    field[:, 8 + by, :] = jnp.where(qy == gy - 1, 0.0, rim_high)

    def prepare(x, _):
        here = f_ref[x].astype(f32)
        field[x, 8 : 8 + by, :] = here
        slope[x] = field[x, 9 : 9 + by, :] - field[x, 7 : 7 + by, :]
        misfit[x] = here - d_ref[x].astype(f32)
        return 0

    lax.fori_loop(0, bx, prepare, 0, unroll=4)
    move.wait()
    quarter = lax.broadcasted_iota(jnp.int32, (8, 8, bz), 2) // (bz // 4)
    for n, ref in enumerate((ra_ref, rb_ref)):
        for tile in range(CAP // 4):
            held = ref[tile * 8 : tile * 8 + 8].astype(f32).reshape(64, bz)
            for k in range(4):
                listed = list_ref[2 + n, tile * 4 + k]
                block = jnp.maximum(listed, 0)
                turned = pltpu.roll(held, ((block - k) & 3) * (bz // 4), 1).reshape(8, 8, bz)
                here = quarter == jnp.where(listed < 0, -1, block & 3)
                planes = pl.ds((block >> 4) * 8, 8)
                start = ((block >> 2) & 3) * 8
                at = pl.ds(pl.multiple_of(start, 8), 8)
                at_f = pl.ds(pl.multiple_of(start + 8, 8), 8)
                misfit[planes, at, :] = jnp.where(here, field[planes, at_f, :] - turned, misfit[planes, at, :])
    for i, x in enumerate((0, bx - 1)):
        edge[2 * i] = slope[x]
        edge[2 * i + 1] = misfit[x]

    def group(g, _):
        rows = pl.ds(pl.multiple_of(g * 8, 8), 8)
        rows_f = pl.ds(pl.multiple_of(g * 8 + 8, 8), 8)
        found = []
        for e in range(2):
            first = e * E + (1 if e == 0 else 0)
            last = e * E + E - (2 if e == 1 else 1)
            before, now = field[first - 1, rows_f, :], field[first, rows_f, :]
            tot = [[jnp.zeros((8, bz), f32) for _ in range(3)] for _ in range(6)]
            right = [[jnp.zeros((8, bz), f32) for _ in range(2)] for _ in range(3)]
            for x in range(first, last + 1):
                after = field[x + 1, rows_f, :]
                grad = (after - before, slope[x, rows, :], along_lanes(now, lane))
                for n, (c, d) in enumerate(PAIRS):
                    tot[n][0] = tot[n][0] + grad[c] * grad[d]
                    tot[n][1] = tot[n][1] + tot[n][0]
                    tot[n][2] = tot[n][2] + tot[n][1]
                miss = misfit[x, rows, :]
                for c in range(3):
                    right[c][0] = right[c][0] + grad[c] * miss
                    right[c][1] = right[c][1] + right[c][0]
                before, now = now, after
            if e == 1:
                for n in range(6):
                    tot[n][1] = tot[n][1] + tot[n][0]
                    tot[n][2] = tot[n][2] + tot[n][1]
                for c in range(3):
                    right[c][1] = right[c][1] + right[c][0]
            ent = []
            for n in range(6):
                a0, a1, a2 = tot[n]
                sq = 2.0 * a2 - a1
                ent.append((sq * (1 / 256), (16.0 * a1 - sq) * (1 / 256), a0 - a1 * (1 / 8) + sq * (1 / 256)))
            rh = [(right[c][1] * (1 / 16), right[c][0] - right[c][1] * (1 / 16)) for c in range(3)]
            found.append((ent, rh))
        for s in range(2):
            for c in range(3):
                e0, e1 = found[0][0][s * 3 + c], found[1][0][s * 3 + c]
                same = (e0[0], e0[2] + e1[0], e1[2])
                cross = (e0[1], e1[1], jnp.zeros((8, bz), f32))
                for ix in range(3):
                    at = slice((c * 3 + ix) * bz, (c * 3 + ix + 1) * bz)
                    moment[pl.ds(pl.multiple_of(s * 64 + g * 8, 8), 8), at] = same[ix]
                    moment[pl.ds(pl.multiple_of(s * 64 + 32 + g * 8, 8), 8), at] = cross[ix]
        for c in range(3):
            r0, r1 = found[0][1][c], found[1][1][c]
            for ix, value in enumerate((r0[0], r0[1] + r1[0], r1[1])):
                at = slice((c * 3 + ix) * bz, (c * 3 + ix + 1) * bz)
                moment[pl.ds(pl.multiple_of(128 + g * 8, 8), 8), at] = value
        return 0

    lax.fori_loop(0, by // 8, group, 0)


def finish_kernel(gx, f_ref, xa_ref, xb_ref, edge, moment, w_ref, z_ref, out_ref):
    px = lax.axis_index("gx")
    even_x = lax.rem(px, 2) == 0
    bx, by, bz = f_ref.shape
    f32 = jnp.float32
    low = jnp.where(px == 0, 0.0, jnp.where(even_x, xb_ref[...], xa_ref[...]).astype(f32))
    high = jnp.where(px == gx - 1, 0.0, jnp.where(even_x, xa_ref[...], xb_ref[...]).astype(f32))
    lane = lax.broadcasted_iota(jnp.int32, (by, bz), 1)
    planes = []
    for i, (x, before, after) in enumerate(((0, low, f_ref[1].astype(f32)), (bx - 1, f_ref[bx - 2].astype(f32), high))):
        grad = (after - before, edge[2 * i], along_lanes(f_ref[x].astype(f32), lane))
        planes.append(([grad[c] * grad[d] for c, d in PAIRS], [grad[c] * edge[2 * i + 1] for c in range(3)]))
    w = w_ref[...]
    along_y = []
    for c in range(3):
        tiles = []
        for ix in range(3):
            tile = moment[:, (c * 3 + ix) * bz : (c * 3 + ix + 1) * bz]
            pieces = []
            for s in range(2):
                first, last = planes[0][0][s * 3 + c], planes[1][0][s * 3 + c]
                same, cross = tile[s * 64 : s * 64 + 32], tile[s * 64 + 32 : s * 64 + 64]
                if ix == 0:
                    same = same + first
                elif ix == 1:
                    same, cross = same + last * (1 / 256), cross + last * (15 / 256)
                else:
                    same = same + last * (225 / 256)
                pieces += [same, cross]
            first, last = planes[0][1][c], planes[1][1][c]
            pieces.append(tile[128:160] + (first, last * (1 / 16), last * (15 / 16))[ix])
            tiles.append(jnp.concatenate(pieces, axis=0))
        sums = 0.0
        for part in split3(jnp.concatenate(tiles, axis=1)):
            sums = sums + jnp.dot(w, part, preferred_element_type=f32)
        along_y.append(sums)
    stacked = jnp.concatenate(
        [along_y[c][(24 if ix == 2 else 0) : (48 if ix == 2 else 24), ix * bz : (ix + 1) * bz] for c in range(3) for ix in range(3)],
        axis=0,
    )
    z = z_ref[...]
    along_z = 0.0
    for part in split3(stacked):
        along_z = along_z + jnp.dot(part, z, preferred_element_type=f32)

    slot = lax.broadcasted_iota(jnp.int32, (8, bz), 1) // NZN
    row = lax.broadcasted_iota(jnp.int32, (8, bz), 0)
    rows_out = [jnp.zeros((8, bz), f32) for _ in range(3)]

    def place(group_at, value, src, dst, mask=None):
        shift = ((dst - src) * NZN) % bz
        moved = pltpu.roll(value, shift, 1) if shift else value
        keep = slot == dst
        if mask is not None:
            keep = keep & mask
        rows_out[group_at] = jnp.where(keep, moved, rows_out[group_at])

    for c in range(3):
        for ix in range(2):
            at = (c * 3 + ix) * 24
            base = c * 4 + ix * 2
            v0, v1, v2 = (along_z[at + i * 8 : at + i * 8 + 8] for i in range(3))
            for tz in range(2):
                place(tz, v0, tz, base)
                place(tz, v1, tz, base + 1)
                place(2, v2, tz, base + tz, row < 4)
            place(2, v2, 2, base, (row >= 4) & (row < 7))
        at = (c * 3 + 2) * 24
        v0, v1, v2 = (along_z[at + i * 8 : at + i * 8 + 8] for i in range(3))
        for tz in range(2):
            place(c, v0, tz, 12 + tz, (row < 4) if c == 2 else None)
            place(2, v1, tz, c * 4 + tz, row == 7)
            place(2, v2, tz, c * 4 + 2 + tz, row == 7)
        place(2, v1, 2, c * 4 + 1, (row >= 4) & (row < 7))
        if c == 2:
            for tz in range(2):
                place(2, v0, tz, 12 + tz, row >= 4)
    for i in range(3):
        for copy in range(out_ref.shape[0]):
            out_ref[copy, i * 8 : i * 8 + 8, :] = rows_out[i]


def solve_kernel(gx, gy, mine_ref, other_ref, up_ref, res_ref, table, vectors):
    count, half, step = gx * gy, gx * gy // 2, gy // 2
    px, qy = lax.axis_index("gx"), lax.axis_index("gy")
    odd = lax.rem(qy, 2)
    f32 = jnp.float32
    shape = (count, 128)
    lane = lax.broadcasted_iota(jnp.int32, shape, 1)
    device = lax.broadcasted_iota(jnp.int32, shape, 0)
    core = device >= half
    place = jnp.where(core, device - half, device)
    chip = lax.rem(place, step)
    slot = lane // NZN
    own = lane < OWN
    ix1 = lax.rem(slot, 4) >= 2
    iy1 = lax.rem(slot, 2) == 1
    corner = own & (lax.rem(slot, 4) == 0)
    y_low = own & ~iy1
    first_p, last_p = place < step, place >= half - step
    first_q, last_q = (chip == 0) & ~core, (chip == step - 1) & core
    is_odd = jnp.full((half, 128), odd, jnp.int32) == 1

    def row(r):
        a, b = mine_ref[pl.ds(r, half, stride=24), :], other_ref[pl.ds(r, half, stride=24), :]
        return jnp.concatenate([jnp.where(is_odd, b, a), jnp.where(is_odd, a, b)], axis=0)

    rows = [row(r) for r in range(24)]

    def lanes(value, shift):
        shift = shift % 128
        return pltpu.roll(value, shift, 1) if shift else value

    def down(value, shift):
        shift = shift % value.shape[0]
        return pltpu.roll(value, shift, 0) if shift else value

    def next_x(value, sign):
        return down(value, -sign * step)

    def next_y(value, sign):
        low, high = value[:half], value[half:]
        if sign > 0:
            return jnp.concatenate([high, down(low, -1)], axis=0)
        return jnp.concatenate([down(high, 1), low], axis=0)

    def from_below_x(value):
        return jnp.where(first_p, 0.0, next_x(value, -1))

    def from_below_y(value):
        return jnp.where(first_q, 0.0, next_y(value, -1))

    def slots(value, src, dst):
        return lanes(value, (dst - src) * NZN)

    def xp(v):
        return jnp.where(ix1, next_x(lanes(v, 18), 1), lanes(v, -18))

    def xm(v):
        return jnp.where(ix1, lanes(v, 18), next_x(lanes(v, -18), -1))

    def yp(v):
        return jnp.where(iy1, next_y(lanes(v, 9), 1), lanes(v, -9))

    def ym(v):
        return jnp.where(iy1, lanes(v, 9), next_y(lanes(v, -9), -1))

    def turn(v, j):
        if j == 1:
            return jnp.where(lane < 72, lanes(v, -36), lanes(v, 72))
        return jnp.where(lane < 36, lanes(v, -72), lanes(v, 36))

    for s in range(2):
        for tx in range(2):
            for ty in range(2):
                for tz in range(2):
                    entry = jnp.where(own, rows[tz * 8 + s * 4 + tx * 2 + ty], 0.0)
                    if ty == 0:
                        spill = slots(rows[16 + s * 2 + tx], tz, 0)
                        entry = entry + from_below_y(jnp.where(y_low, spill, 0.0))
                    if tx == 0:
                        spill = jnp.zeros(shape, f32)
                        for c in range(3):
                            for iy in range(2):
                                moved = slots(rows[c * 8 + iy * 4 + s * 2 + ty], 12 + tz, c * 4 + iy)
                                spill = jnp.where(slot == c * 4 + iy, moved, spill)
                        if ty == 0:
                            both = slots(rows[23], s * 2 + tz, 0)
                            spill = spill + from_below_y(jnp.where(corner, both, 0.0))
                        entry = entry + from_below_x(spill)
                    if tx == 1:
                        entry = jnp.where(last_p & ix1, 0.0, entry)
                    if ty == 1:
                        entry = jnp.where(last_q & iy1, 0.0, entry)
                    kind = tx * 4 + ty * 2 + tz
                    if s == 0:
                        table[kind] = entry
                    else:
                        table[8 + kind] = jnp.where(own, turn(entry, 2), 0.0)
                        table[16 + kind] = entry

    r0, r1, r2 = rows[20], rows[21], rows[22]
    rhs = jnp.where(iy1, lanes(r1, 9), r0) + from_below_y(jnp.where(iy1, 0.0, r2))
    far = jnp.where(iy1, r1, lanes(r0, -9)) + from_below_y(jnp.where(iy1, 0.0, lanes(r2, -9)))
    rhs = rhs + from_below_x(jnp.where(ix1, 0.0, far))
    rhs = jnp.where(own, rhs, 0.0)

    def operate(v):
        upper = [v, lanes(v, -1)]
        upper += [yp(u) for u in upper]
        upper += [xp(u) for u in upper]
        parts = []
        for s in range(3):
            low = []
            for to in range(8):
                found = 0.0
                for up in range(8):
                    if up & to == 0:
                        found = found + table[8 * s + (up | to)] * upper[up]
                low.append(found)
            by_z = [low[2 * i] + lanes(low[2 * i + 1], 1) for i in range(4)]
            by_y = [by_z[2 * i] + ym(by_z[2 * i + 1]) for i in range(2)]
            parts.append(by_y[0] + xm(by_y[1]))
        coupled = parts[0] + turn(parts[1], 1) + turn(parts[2], 2)
        return damping * v + jnp.where(own, coupled, 0.0)

    def total(v):
        return jnp.sum(jnp.sum(v, axis=0, keepdims=True), axis=1, keepdims=True)

    def iterate(state):
        update, residual, direction, norm_now = state
        image = operate(direction)
        alpha = norm_now / total(direction * image)
        update = update + alpha * direction
        residual = residual - alpha * image
        norm_next = total(residual * residual)
        direction = residual + (norm_next / norm_now) * direction
        return update, residual, direction, norm_next

    start = (jnp.zeros(shape, f32), rhs, rhs, total(rhs * rhs))
    for _ in range(ITERS):
        start = iterate(start)
    update, residual, _, _ = start
    vectors[0] = update
    vectors[1] = residual
    me = odd * half + px * step + qy // 2
    for i, ref in enumerate((up_ref, res_ref)):
        line = vectors[i, pl.ds(me, 1), :]
        for c in range(3):
            for ix in range(2):
                for iy in range(2):
                    ref[c, ix, iy : iy + 1, :] = lanes(line, -(c * 4 + ix * 2 + iy) * NZN)[:, :NZN]


LIMIT = 24 * 2**20
HBM = pl.BlockSpec(memory_space=pltpu.MemorySpace.HBM)
VMEM = pl.BlockSpec(memory_space=pltpu.VMEM)


def exchange(value, gx, gy, axis, start):
    def partner(p, q):
        at, count = (p, gx) if axis == "gx" else (q, gy)
        other = at + 1 if (at - start) % 2 == 0 else at - 1
        if 0 <= other < count:
            return (other, q) if axis == "gx" else (p, other)
        return (p, q ^ 1) if axis == "gx" else (p ^ 1, q)

    pairs = []
    for p in range(gx):
        for q in range(gy):
            to = partner(p, q)
            pairs.append((p * gy + q, to[0] * gy + to[1]))
    return lax.ppermute(value, ("gx", "gy"), pairs)


def local(reference_scan, deformed_scan, source_column):
    bx, by, bz = reference_scan.shape
    gx, gy = lax.axis_size("gx"), lax.axis_size("gy")
    half = jnp.bfloat16
    table = source_column[0, :, :, 0]
    sub = 8
    split = (bx, by // sub, sub, bz)
    packed = jax.ShapeDtypeStruct((CAP * 2 + bx // sub, sub, bz), half)
    plane = jax.ShapeDtypeStruct((by // sub, sub, bz), half)
    whole = jax.ShapeDtypeStruct(split, half)
    ya, yb, xa, xb, near, moving, lists = pl.pallas_call(
        functools.partial(pack_kernel, gy),
        out_shape=[packed, packed, plane, plane, whole, whole, jax.ShapeDtypeStruct((8, 128), jnp.int32)],
        in_specs=[HBM] * 3,
        out_specs=[VMEM] * 7,
        scratch_shapes=[
            pltpu.VMEM(table.shape, jnp.int32),
            pltpu.SemaphoreType.DMA((2, CHUNKS)),
            pltpu.SemaphoreType.DMA,
        ],
        compiler_params=pltpu.CompilerParams(vmem_limit_bytes=LIMIT),
        name="pack",
    )(*(pltpu.with_memory_space_constraint(value, pltpu.MemorySpace.HBM) for value in (reference_scan.reshape(split), deformed_scan.reshape(split), table)))
    rb = exchange(yb, gx, gy, "gy", 1)
    xb = exchange(xb, gx, gy, "gx", 1)
    xa = exchange(xa, gx, gy, "gx", 0)
    ra = exchange(ya, gx, gy, "gy", 0)
    xa, xb = xa.reshape(by, bz), xb.reshape(by, bz)
    near, moving = near.reshape(bx, by, bz), moving.reshape(bx, by, bz)
    moment, edge = pl.pallas_call(
        functools.partial(interior_kernel, gy),
        out_shape=[jax.ShapeDtypeStruct((160, 9 * bz), jnp.float32), jax.ShapeDtypeStruct((4, by, bz), jnp.float32)],
        in_specs=[VMEM] * 5,
        out_specs=[VMEM] * 2,
        scratch_shapes=[
            pltpu.VMEM((bx, by + 16, bz), jnp.float32),
            pltpu.VMEM((bx, by, bz), jnp.float32),
            pltpu.VMEM((bx, by, bz), jnp.float32),
            pltpu.SMEM((8, 128), jnp.int32),
            pltpu.SemaphoreType.DMA,
        ],
        compiler_params=pltpu.CompilerParams(vmem_limit_bytes=LIMIT),
        cost_estimate=pl.CostEstimate(flops=8_000_000, bytes_accessed=2_000_000, transcendentals=0),
        name="interior",
    )(near, moving, ra, rb, lists)
    w, z = weights()
    payload = pl.pallas_call(
        functools.partial(finish_kernel, gx),
        out_shape=jax.ShapeDtypeStruct((gx * gy // 2, 24, bz), jnp.float32),
        in_specs=[VMEM] * 7,
        out_specs=VMEM,
        compiler_params=pltpu.CompilerParams(vmem_limit_bytes=LIMIT),
        name="finish",
    )(near, xa, xb, edge, moment, jnp.asarray(w, half), jnp.asarray(z, half))
    groups = [[i * 2 + core for i in range(gx * gy // 2)] for core in range(2)]
    mine = lax.all_to_all(payload, ("gx", "gy"), 0, 0, axis_index_groups=groups)
    other = lax.ppermute(mine, "gy", [(i, i ^ 1) for i in range(gy)])
    out = jax.ShapeDtypeStruct((3, 2, 2, NZN), jnp.float32)
    update, residual = pl.pallas_call(
        functools.partial(solve_kernel, gx, gy),
        out_shape=[out, out],
        in_specs=[VMEM] * 2,
        out_specs=[VMEM] * 2,
        scratch_shapes=[
            pltpu.VMEM((24, gx * gy, bz), jnp.float32),
            pltpu.VMEM((2, gx * gy, bz), jnp.float32),
        ],
        compiler_params=pltpu.CompilerParams(vmem_limit_bytes=LIMIT),
        name="solve",
    )(mine.reshape(-1, bz), other.reshape(-1, bz))
    return update, residual


def solution(mesh):
    return jax.shard_map(
        local,
        mesh=mesh,
        in_specs=(P("gx", "gy", None), P("gx", "gy", None), P("gx", None, None, None)),
        out_specs=(P(None, "gx", "gy", None), P(None, "gx", "gy", None)),
        check_vma=False,
    )
```

```python
import functools

import jax
import jax.numpy as jnp
import numpy as np
from jax import lax
from jax.experimental import pallas as pl
from jax.experimental.pallas import tpu as pltpu
from jax.sharding import PartitionSpec as P


E = 16
ITERS = 4
NZN = 9
CAP = 16
BLOCKS = 64
CHUNKS = 2
OWN = 12 * NZN


damping = 0.1


def weights():
    m = np.arange(E, 0, -1, dtype=np.float64) / E
    same_low, cross, same_high, low, high = m * m, m * (1 - m), (1 - m) ** 2, m, 1 - m

    def along(count):
        d = np.zeros((count + 1, count * E))
        o = np.zeros((count + 1, count * E))
        h = np.zeros((count + 1, count * E))
        for e in range(count):
            at = slice(e * E, (e + 1) * E)
            d[e, at] += same_low
            d[e + 1, at] += same_high
            o[e, at] += cross
            h[e, at] += low
            h[e + 1, at] += high
        return d, o, h

    yd, yo, yh = along(2)
    w = np.zeros((48, 160))
    for s in range(2):
        for tx in range(2):
            k = slice((s * 2 + tx) * 32, (s * 2 + tx) * 32 + 32)
            for iy in range(2):
                w[iy * 8 + s * 4 + tx * 2 + 0, k] = yd[iy]
                w[iy * 8 + s * 4 + tx * 2 + 1, k] = yo[iy]
            w[16 + s * 2 + tx, k] = yd[2]
        k = slice(s * 64, s * 64 + 32)
        for iy in range(2):
            w[24 + iy * 4 + s * 2 + 0, k] = yd[iy]
            w[24 + iy * 4 + s * 2 + 1, k] = yo[iy]
        w[(32 if s == 0 else 40) + 7, k] = yd[2]
    for iy in range(3):
        w[20 + iy, 128:160] = yh[iy]
        w[32 + 4 + iy, 128:160] = yh[iy]
    zd, zo, zh = along(8)
    z = np.zeros((128, 128))
    scale = 1.0 / (2.0 * E)
    z[:, 0:9] = zd.T * scale * scale
    z[:, 9:18] = zo.T * scale * scale
    z[:, 18:27] = zh.T * scale
    return w.astype(np.float32), z.astype(np.float32)


def split3(value):
    high = value.astype(jnp.bfloat16)
    rest = value - high.astype(jnp.float32)
    mid = rest.astype(jnp.bfloat16)
    low = (rest - mid.astype(jnp.float32)).astype(jnp.bfloat16)
    return high, mid, low


def neighbours(q):
    even = lax.rem(q, 2) == 0
    return jnp.where(even, q + 1, q - 1), jnp.where(even, q - 1, q + 1)


def block_lists(table, q, gy):
    first, second = neighbours(q)
    own = table[pl.ds(q, 1), :]
    match = [table[pl.ds(jnp.clip(to, 0, gy - 1), 1), :] == q for to in (first, second)] + [own == to for to in (first, second)]
    match = jnp.concatenate([m.astype(jnp.float32) for m in match] * 2, axis=0).astype(jnp.bfloat16)
    row = lax.broadcasted_iota(jnp.int32, (BLOCKS, BLOCKS), 0)
    col = lax.broadcasted_iota(jnp.int32, (BLOCKS, BLOCKS), 1)

    def against(matrix):
        matrix = matrix.astype(jnp.float32).astype(jnp.bfloat16)
        return lax.dot_general(matrix, match, (((1,), (1,)), ((), ())), preferred_element_type=jnp.float32)

    rank, taken = against(col < row), against(col == row)
    slot = lax.broadcasted_iota(jnp.int32, (BLOCKS, 128), 1).astype(jnp.float32)
    number = (lax.broadcasted_iota(jnp.int32, (BLOCKS, 128), 0) + 1).astype(jnp.float32)
    rows = []
    for i in range(4):
        here = (rank[:, i : i + 1] == slot) & (taken[:, i : i + 1] > 0.5)
        rows.append(jnp.sum(jnp.where(here, number, 0.0), axis=0, keepdims=True))
    return (jnp.concatenate(rows * 2, axis=0) - 1.0).astype(jnp.int32)


def pack_kernel(gy, f_hbm, d_hbm, col_hbm, ya_ref, yb_ref, xa_ref, xb_ref, f_ref, d_ref, lists, col_ref, sems, sem):
    even_x = lax.rem(lax.axis_index("gx"), 2) == 0
    q = lax.axis_index("gy")
    even_y = lax.rem(q, 2) == 0
    bx, groups, sub, bz = f_hbm.shape
    chunk = bx // CHUNKS
    fetch = pltpu.make_async_copy(col_hbm, col_ref, sem)
    fetch.start()
    copies = []
    for n, (src, dst) in enumerate(((d_hbm, d_ref), (f_hbm, f_ref))):
        for i in range(CHUNKS):
            at = pl.ds(i * chunk, chunk)
            copies.append(pltpu.make_async_copy(src.at[at], dst.at[at], sems.at[n, i]))
    for copy in copies[:CHUNKS]:
        copy.start()
    fetch.wait()
    found = block_lists(col_ref, q, gy)
    lists[...] = found
    for copy in copies[CHUNKS:]:
        copy.start()
    for copy in copies[:CHUNKS]:
        copy.wait()
    quarter = lax.broadcasted_iota(jnp.int32, (64, bz), 1) // (bz // 4)
    for n, ref in enumerate((ya_ref, yb_ref)):
        for tile in range(CAP // 4):
            held = jnp.zeros((64, bz), jnp.float32)
            for k in range(4):
                block = jnp.maximum(found[n, tile * 4 + k], 0)
                piece = d_ref[pl.ds((block >> 4) * 8, 8), (block >> 2) & 3].astype(jnp.float32).reshape(64, bz)
                turned = pltpu.roll(piece, ((k - block) & 3) * (bz // 4), 1)
                held = jnp.where(quarter == k, turned, held)
            ref[tile * 8 : tile * 8 + 8] = held.astype(jnp.bfloat16).reshape(8, sub, bz)
    for copy in copies[CHUNKS:]:
        copy.wait()
    head, tail = f_ref[:, 0, 0, :], f_ref[:, groups - 1, sub - 1, :]
    ya_ref[CAP * 2 :] = jnp.where(even_y, tail, head).reshape(bx // sub, sub, bz)
    yb_ref[CAP * 2 :] = jnp.where(even_y, head, tail).reshape(bx // sub, sub, bz)
    first, last = f_ref[0], f_ref[bx - 1]
    xa_ref[...] = jnp.where(even_x, last, first)
    xb_ref[...] = jnp.where(even_x, first, last)


PAIRS = ((0, 0), (1, 1), (2, 2), (0, 1), (1, 2), (2, 0))


def along_lanes(now, lane):
    size = now.shape[-1]
    up = jnp.where(lane == size - 1, 0.0, pltpu.roll(now, size - 1, 1))
    return up - jnp.where(lane == 0, 0.0, pltpu.roll(now, 1, 1))


def interior_kernel(gy, f_ref, d_ref, ra_ref, rb_ref, lists, moment, edge, field, slope, misfit, list_ref, sem):
    move = pltpu.make_async_copy(lists, list_ref, sem)
    move.start()
    qy = lax.axis_index("gy")
    even_y = lax.rem(qy, 2) == 0
    bx, by, bz = f_ref.shape
    f32 = jnp.float32
    lane = lax.broadcasted_iota(jnp.int32, (8, bz), 1)
    rim_a, rim_b = (ref[CAP * 2 :].astype(f32).reshape(bx, bz) for ref in (ra_ref, rb_ref))
    rim_low, rim_high = jnp.where(even_y, rim_b, rim_a), jnp.where(even_y, rim_a, rim_b)
    field[:, 7, :] = jnp.where(qy == 0, 0.0, rim_low)
    field[:, 8 + by, :] = jnp.where(qy == gy - 1, 0.0, rim_high)

    def prepare(x, _):
        here = f_ref[x].astype(f32)
        field[x, 8 : 8 + by, :] = here
        slope[x] = field[x, 9 : 9 + by, :] - field[x, 7 : 7 + by, :]
        misfit[x] = here - d_ref[x].astype(f32)
        return 0

    lax.fori_loop(0, bx, prepare, 0, unroll=4)
    move.wait()
    quarter = lax.broadcasted_iota(jnp.int32, (8, 8, bz), 2) // (bz // 4)
    for n, ref in enumerate((ra_ref, rb_ref)):
        for tile in range(CAP // 4):
            held = ref[tile * 8 : tile * 8 + 8].astype(f32).reshape(64, bz)
            for k in range(4):
                listed = list_ref[2 + n, tile * 4 + k]
                block = jnp.maximum(listed, 0)
                turned = pltpu.roll(held, ((block - k) & 3) * (bz // 4), 1).reshape(8, 8, bz)
                here = quarter == jnp.where(listed < 0, -1, block & 3)
                planes = pl.ds((block >> 4) * 8, 8)
                start = ((block >> 2) & 3) * 8
                at = pl.ds(pl.multiple_of(start, 8), 8)
                at_f = pl.ds(pl.multiple_of(start + 8, 8), 8)
                misfit[planes, at, :] = jnp.where(here, field[planes, at_f, :] - turned, misfit[planes, at, :])
    for i, x in enumerate((0, bx - 1)):
        edge[2 * i] = slope[x]
        edge[2 * i + 1] = misfit[x]

    def group(g, _):
        rows = pl.ds(pl.multiple_of(g * 8, 8), 8)
        rows_f = pl.ds(pl.multiple_of(g * 8 + 8, 8), 8)
        found = []
        for e in range(2):
            first = e * E + (1 if e == 0 else 0)
            last = e * E + E - (2 if e == 1 else 1)
            before, now = field[first - 1, rows_f, :], field[first, rows_f, :]
            tot = [[jnp.zeros((8, bz), f32) for _ in range(3)] for _ in range(6)]
            right = [[jnp.zeros((8, bz), f32) for _ in range(2)] for _ in range(3)]
            for x in range(first, last + 1):
                after = field[x + 1, rows_f, :]
                grad = (after - before, slope[x, rows, :], along_lanes(now, lane))
                for n, (c, d) in enumerate(PAIRS):
                    tot[n][0] = tot[n][0] + grad[c] * grad[d]
                    tot[n][1] = tot[n][1] + tot[n][0]
                    tot[n][2] = tot[n][2] + tot[n][1]
                miss = misfit[x, rows, :]
                for c in range(3):
                    right[c][0] = right[c][0] + grad[c] * miss
                    right[c][1] = right[c][1] + right[c][0]
                before, now = now, after
            if e == 1:
                for n in range(6):
                    tot[n][1] = tot[n][1] + tot[n][0]
                    tot[n][2] = tot[n][2] + tot[n][1]
                for c in range(3):
                    right[c][1] = right[c][1] + right[c][0]
            ent = []
            for n in range(6):
                a0, a1, a2 = tot[n]
                sq = 2.0 * a2 - a1
                ent.append((sq * (1 / 256), (16.0 * a1 - sq) * (1 / 256), a0 - a1 * (1 / 8) + sq * (1 / 256)))
            rh = [(right[c][1] * (1 / 16), right[c][0] - right[c][1] * (1 / 16)) for c in range(3)]
            found.append((ent, rh))
        for s in range(2):
            for c in range(3):
                e0, e1 = found[0][0][s * 3 + c], found[1][0][s * 3 + c]
                same = (e0[0], e0[2] + e1[0], e1[2])
                cross = (e0[1], e1[1], jnp.zeros((8, bz), f32))
                for ix in range(3):
                    at = slice((c * 3 + ix) * bz, (c * 3 + ix + 1) * bz)
                    moment[pl.ds(pl.multiple_of(s * 64 + g * 8, 8), 8), at] = same[ix]
                    moment[pl.ds(pl.multiple_of(s * 64 + 32 + g * 8, 8), 8), at] = cross[ix]
        for c in range(3):
            r0, r1 = found[0][1][c], found[1][1][c]
            for ix, value in enumerate((r0[0], r0[1] + r1[0], r1[1])):
                at = slice((c * 3 + ix) * bz, (c * 3 + ix + 1) * bz)
                moment[pl.ds(pl.multiple_of(128 + g * 8, 8), 8), at] = value
        return 0

    lax.fori_loop(0, by // 8, group, 0)


def finish_kernel(gx, f_ref, xa_ref, xb_ref, edge, moment, w_ref, z_ref, out_ref):
    px = lax.axis_index("gx")
    even_x = lax.rem(px, 2) == 0
    bx, by, bz = f_ref.shape
    f32 = jnp.float32
    low = jnp.where(px == 0, 0.0, jnp.where(even_x, xb_ref[...], xa_ref[...]).astype(f32))
    high = jnp.where(px == gx - 1, 0.0, jnp.where(even_x, xa_ref[...], xb_ref[...]).astype(f32))
    lane = lax.broadcasted_iota(jnp.int32, (by, bz), 1)
    planes = []
    for i, (x, before, after) in enumerate(((0, low, f_ref[1].astype(f32)), (bx - 1, f_ref[bx - 2].astype(f32), high))):
        grad = (after - before, edge[2 * i], along_lanes(f_ref[x].astype(f32), lane))
        planes.append(([grad[c] * grad[d] for c, d in PAIRS], [grad[c] * edge[2 * i + 1] for c in range(3)]))
    w = w_ref[...]
    along_y = []
    for c in range(3):
        tiles = []
        for ix in range(3):
            tile = moment[:, (c * 3 + ix) * bz : (c * 3 + ix + 1) * bz]
            pieces = []
            for s in range(2):
                first, last = planes[0][0][s * 3 + c], planes[1][0][s * 3 + c]
                same, cross = tile[s * 64 : s * 64 + 32], tile[s * 64 + 32 : s * 64 + 64]
                if ix == 0:
                    same = same + first
                elif ix == 1:
                    same, cross = same + last * (1 / 256), cross + last * (15 / 256)
                else:
                    same = same + last * (225 / 256)
                pieces += [same, cross]
            first, last = planes[0][1][c], planes[1][1][c]
            pieces.append(tile[128:160] + (first, last * (1 / 16), last * (15 / 16))[ix])
            tiles.append(jnp.concatenate(pieces, axis=0))
        sums = 0.0
        for part in split3(jnp.concatenate(tiles, axis=1)):
            sums = sums + jnp.dot(w, part, preferred_element_type=f32)
        along_y.append(sums)
    stacked = jnp.concatenate(
        [along_y[c][(24 if ix == 2 else 0) : (48 if ix == 2 else 24), ix * bz : (ix + 1) * bz] for c in range(3) for ix in range(3)],
        axis=0,
    )
    z = z_ref[...]
    along_z = 0.0
    for part in split3(stacked):
        along_z = along_z + jnp.dot(part, z, preferred_element_type=f32)

    slot = lax.broadcasted_iota(jnp.int32, (8, bz), 1) // NZN
    row = lax.broadcasted_iota(jnp.int32, (8, bz), 0)
    rows_out = [jnp.zeros((8, bz), f32) for _ in range(3)]

    def place(group_at, value, src, dst, mask=None):
        shift = ((dst - src) * NZN) % bz
        moved = pltpu.roll(value, shift, 1) if shift else value
        keep = slot == dst
        if mask is not None:
            keep = keep & mask
        rows_out[group_at] = jnp.where(keep, moved, rows_out[group_at])

    for c in range(3):
        for ix in range(2):
            at = (c * 3 + ix) * 24
            base = c * 4 + ix * 2
            v0, v1, v2 = (along_z[at + i * 8 : at + i * 8 + 8] for i in range(3))
            for tz in range(2):
                place(tz, v0, tz, base)
                place(tz, v1, tz, base + 1)
                place(2, v2, tz, base + tz, row < 4)
            place(2, v2, 2, base, (row >= 4) & (row < 7))
        at = (c * 3 + 2) * 24
        v0, v1, v2 = (along_z[at + i * 8 : at + i * 8 + 8] for i in range(3))
        for tz in range(2):
            place(c, v0, tz, 12 + tz, (row < 4) if c == 2 else None)
            place(2, v1, tz, c * 4 + tz, row == 7)
            place(2, v2, tz, c * 4 + 2 + tz, row == 7)
        place(2, v1, 2, c * 4 + 1, (row >= 4) & (row < 7))
        if c == 2:
            for tz in range(2):
                place(2, v0, tz, 12 + tz, row >= 4)
    for i in range(3):
        for copy in range(out_ref.shape[0]):
            out_ref[copy, i * 8 : i * 8 + 8, :] = rows_out[i]


def solve_kernel(gx, gy, mine_ref, other_ref, up_ref, res_ref, table, vectors):
    count, half, step = gx * gy, gx * gy // 2, gy // 2
    px, qy = lax.axis_index("gx"), lax.axis_index("gy")
    odd = lax.rem(qy, 2)
    f32 = jnp.float32
    shape = (count, 128)
    lane = lax.broadcasted_iota(jnp.int32, shape, 1)
    device = lax.broadcasted_iota(jnp.int32, shape, 0)
    core = device >= half
    place = jnp.where(core, device - half, device)
    chip = lax.rem(place, step)
    slot = lane // NZN
    own = lane < OWN
    ix1 = lax.rem(slot, 4) >= 2
    iy1 = lax.rem(slot, 2) == 1
    corner = own & (lax.rem(slot, 4) == 0)
    y_low = own & ~iy1
    first_p, last_p = place < step, place >= half - step
    first_q, last_q = (chip == 0) & ~core, (chip == step - 1) & core
    is_odd = jnp.full((half, 128), odd, jnp.int32) == 1

    def row(r):
        a, b = mine_ref[pl.ds(r, half, stride=24), :], other_ref[pl.ds(r, half, stride=24), :]
        return jnp.concatenate([jnp.where(is_odd, b, a), jnp.where(is_odd, a, b)], axis=0)

    rows = [row(r) for r in range(24)]

    def lanes(value, shift):
        shift = shift % 128
        return pltpu.roll(value, shift, 1) if shift else value

    def down(value, shift):
        shift = shift % value.shape[0]
        return pltpu.roll(value, shift, 0) if shift else value

    def next_x(value, sign):
        return down(value, -sign * step)

    def next_y(value, sign):
        low, high = value[:half], value[half:]
        if sign > 0:
            return jnp.concatenate([high, down(low, -1)], axis=0)
        return jnp.concatenate([down(high, 1), low], axis=0)

    def from_below_x(value):
        return jnp.where(first_p, 0.0, next_x(value, -1))

    def from_below_y(value):
        return jnp.where(first_q, 0.0, next_y(value, -1))

    def slots(value, src, dst):
        return lanes(value, (dst - src) * NZN)

    def xp(v):
        return jnp.where(ix1, next_x(lanes(v, 18), 1), lanes(v, -18))

    def xm(v):
        return jnp.where(ix1, lanes(v, 18), next_x(lanes(v, -18), -1))

    def yp(v):
        return jnp.where(iy1, next_y(lanes(v, 9), 1), lanes(v, -9))

    def ym(v):
        return jnp.where(iy1, lanes(v, 9), next_y(lanes(v, -9), -1))

    def turn(v, j):
        if j == 1:
            return jnp.where(lane < 72, lanes(v, -36), lanes(v, 72))
        return jnp.where(lane < 36, lanes(v, -72), lanes(v, 36))

    spread = {}
    for s in range(2):
        for tx in range(2):
            for ty in range(2):
                for tz in range(2):
                    entry = jnp.where(own, rows[tz * 8 + s * 4 + tx * 2 + ty], 0.0)
                    if ty == 0:
                        spill = slots(rows[16 + s * 2 + tx], tz, 0)
                        entry = entry + from_below_y(jnp.where(y_low, spill, 0.0))
                    if tx == 0:
                        spill = jnp.zeros(shape, f32)
                        for c in range(3):
                            for iy in range(2):
                                key = (c, iy, s, ty)
                                if key not in spread:
                                    spread[key] = slots(rows[c * 8 + iy * 4 + s * 2 + ty], 12, c * 4 + iy)
                                spill = jnp.where(slot == c * 4 + iy + tz, spread[key], spill)
                        spill = slots(spill, tz, 0)
                        if ty == 0:
                            both = slots(rows[23], s * 2 + tz, 0)
                            spill = spill + from_below_y(jnp.where(corner, both, 0.0))
                        entry = entry + from_below_x(spill)
                    if tx == 1:
                        entry = jnp.where(last_p & ix1, 0.0, entry)
                    if ty == 1:
                        entry = jnp.where(last_q & iy1, 0.0, entry)
                    kind = tx * 4 + ty * 2 + tz
                    if s == 0:
                        table[kind] = entry
                    else:
                        table[8 + kind] = jnp.where(own, turn(entry, 2), 0.0)
                        table[16 + kind] = entry

    r0, r1, r2 = rows[20], rows[21], rows[22]
    rhs = jnp.where(iy1, lanes(r1, 9), r0) + from_below_y(jnp.where(iy1, 0.0, r2))
    far = jnp.where(iy1, r1, lanes(r0, -9)) + from_below_y(jnp.where(iy1, 0.0, lanes(r2, -9)))
    rhs = rhs + from_below_x(jnp.where(ix1, 0.0, far))
    rhs = jnp.where(own, rhs, 0.0)

    def operate(v):
        upper = [v, lanes(v, -1)]
        upper += [yp(u) for u in upper]
        upper += [xp(u) for u in upper]
        parts = []
        for s in range(3):
            low = []
            for to in range(8):
                found = 0.0
                for up in range(8):
                    if up & to == 0:
                        found = found + table[8 * s + (up | to)] * upper[up]
                low.append(found)
            by_z = [low[2 * i] + lanes(low[2 * i + 1], 1) for i in range(4)]
            by_y = [by_z[2 * i] + ym(by_z[2 * i + 1]) for i in range(2)]
            parts.append(by_y[0] + xm(by_y[1]))
        coupled = parts[0] + turn(parts[1], 1) + turn(parts[2], 2)
        return damping * v + jnp.where(own, coupled, 0.0)

    def total(v):
        return jnp.sum(jnp.sum(v, axis=0, keepdims=True), axis=1, keepdims=True)

    def iterate(state):
        update, residual, direction, norm_now = state
        image = operate(direction)
        alpha = norm_now / total(direction * image)
        update = update + alpha * direction
        residual = residual - alpha * image
        norm_next = total(residual * residual)
        direction = residual + (norm_next / norm_now) * direction
        return update, residual, direction, norm_next

    start = (jnp.zeros(shape, f32), rhs, rhs, total(rhs * rhs))
    for _ in range(ITERS):
        start = iterate(start)
    update, residual, _, _ = start
    vectors[0] = update
    vectors[1] = residual
    me = odd * half + px * step + qy // 2
    for i, ref in enumerate((up_ref, res_ref)):
        line = vectors[i, pl.ds(me, 1), :]
        for c in range(3):
            for ix in range(2):
                for iy in range(2):
                    ref[c, ix, iy : iy + 1, :] = lanes(line, -(c * 4 + ix * 2 + iy) * NZN)[:, :NZN]


LIMIT = 24 * 2**20
HBM = pl.BlockSpec(memory_space=pltpu.MemorySpace.HBM)
VMEM = pl.BlockSpec(memory_space=pltpu.VMEM)


def exchange(value, gx, gy, axis, start):
    def partner(p, q):
        at, count = (p, gx) if axis == "gx" else (q, gy)
        other = at + 1 if (at - start) % 2 == 0 else at - 1
        if 0 <= other < count:
            return (other, q) if axis == "gx" else (p, other)
        return (p, q ^ 1) if axis == "gx" else (p ^ 1, q)

    pairs = []
    for p in range(gx):
        for q in range(gy):
            to = partner(p, q)
            pairs.append((p * gy + q, to[0] * gy + to[1]))
    return lax.ppermute(value, ("gx", "gy"), pairs)


def local(reference_scan, deformed_scan, source_column):
    bx, by, bz = reference_scan.shape
    gx, gy = lax.axis_size("gx"), lax.axis_size("gy")
    half = jnp.bfloat16
    table = source_column[0, :, :, 0]
    sub = 8
    split = (bx, by // sub, sub, bz)
    packed = jax.ShapeDtypeStruct((CAP * 2 + bx // sub, sub, bz), half)
    plane = jax.ShapeDtypeStruct((by // sub, sub, bz), half)
    whole = jax.ShapeDtypeStruct(split, half)
    ya, yb, xa, xb, near, moving, lists = pl.pallas_call(
        functools.partial(pack_kernel, gy),
        out_shape=[packed, packed, plane, plane, whole, whole, jax.ShapeDtypeStruct((8, 128), jnp.int32)],
        in_specs=[HBM] * 3,
        out_specs=[VMEM] * 7,
        scratch_shapes=[
            pltpu.VMEM(table.shape, jnp.int32),
            pltpu.SemaphoreType.DMA((2, CHUNKS)),
            pltpu.SemaphoreType.DMA,
        ],
        compiler_params=pltpu.CompilerParams(vmem_limit_bytes=LIMIT),
        name="pack",
    )(*(pltpu.with_memory_space_constraint(value, pltpu.MemorySpace.HBM) for value in (reference_scan.reshape(split), deformed_scan.reshape(split), table)))
    rb = exchange(yb, gx, gy, "gy", 1)
    xb = exchange(xb, gx, gy, "gx", 1)
    xa = exchange(xa, gx, gy, "gx", 0)
    ra = exchange(ya, gx, gy, "gy", 0)
    xa, xb = xa.reshape(by, bz), xb.reshape(by, bz)
    near, moving = near.reshape(bx, by, bz), moving.reshape(bx, by, bz)
    moment, edge = pl.pallas_call(
        functools.partial(interior_kernel, gy),
        out_shape=[jax.ShapeDtypeStruct((160, 9 * bz), jnp.float32), jax.ShapeDtypeStruct((4, by, bz), jnp.float32)],
        in_specs=[VMEM] * 5,
        out_specs=[VMEM] * 2,
        scratch_shapes=[
            pltpu.VMEM((bx, by + 16, bz), jnp.float32),
            pltpu.VMEM((bx, by, bz), jnp.float32),
            pltpu.VMEM((bx, by, bz), jnp.float32),
            pltpu.SMEM((8, 128), jnp.int32),
            pltpu.SemaphoreType.DMA,
        ],
        compiler_params=pltpu.CompilerParams(vmem_limit_bytes=LIMIT),
        cost_estimate=pl.CostEstimate(flops=8_000_000, bytes_accessed=2_000_000, transcendentals=0),
        name="interior",
    )(near, moving, ra, rb, lists)
    w, z = weights()
    payload = pl.pallas_call(
        functools.partial(finish_kernel, gx),
        out_shape=jax.ShapeDtypeStruct((gx * gy // 2, 24, bz), jnp.float32),
        in_specs=[VMEM] * 7,
        out_specs=VMEM,
        compiler_params=pltpu.CompilerParams(vmem_limit_bytes=LIMIT),
        name="finish",
    )(near, xa, xb, edge, moment, jnp.asarray(w, half), jnp.asarray(z, half))
    groups = [[i * 2 + core for i in range(gx * gy // 2)] for core in range(2)]
    mine = lax.all_to_all(payload, ("gx", "gy"), 0, 0, axis_index_groups=groups)
    other = lax.ppermute(mine, "gy", [(i, i ^ 1) for i in range(gy)])
    out = jax.ShapeDtypeStruct((3, 2, 2, NZN), jnp.float32)
    update, residual = pl.pallas_call(
        functools.partial(solve_kernel, gx, gy),
        out_shape=[out, out],
        in_specs=[VMEM] * 2,
        out_specs=[VMEM] * 2,
        scratch_shapes=[
            pltpu.VMEM((24, gx * gy, bz), jnp.float32),
            pltpu.VMEM((2, gx * gy, bz), jnp.float32),
        ],
        compiler_params=pltpu.CompilerParams(vmem_limit_bytes=LIMIT),
        name="solve",
    )(mine.reshape(-1, bz), other.reshape(-1, bz))
    return update, residual


def solution(mesh):
    return jax.shard_map(
        local,
        mesh=mesh,
        in_specs=(P("gx", "gy", None), P("gx", "gy", None), P("gx", None, None, None)),
        out_specs=(P(None, "gx", "gy", None), P(None, "gx", "gy", None)),
        check_vma=False,
    )
```
